32 devices in a mesh: space: 8 (over y, x, core), group: 4 (over z).
Axes of the slice: x: 2, y: 2, z: 4, core: 2. Of those that a mesh axis runs over, the one named last changes fastest.
Arguments:
- snapshot_basis: bfloat16 [65536, 1024], P('space', 'group'), may hold values from -40 to 40
- sketch: float32 [2, 512, 256], replicated, may hold values from -0.25 to 0.25
Outputs:
- merged_basis: bfloat16 [65536, 256], P(('space', 'group'))
The draws below stay inside these ranges and needn't reach their ends.
All inputs are finite; a program needn't handle non-finite values.
Results may differ from the reference program's by a relative error of at most 0.0067.
Values may be sent and summed in bfloat16 or wider, within the bound.
No kernel may reach another device: no remote copies, remote signals or barrier semaphores. Data moves between devices by JAX's collectives and lax.ppermute only.
A program may use at most 128 MiB of HBM per device.

```python
import jax
import jax.numpy as jnp
from jax import lax

K = 256
STEPS = 5
ROWS_DEV = 8192
ROWS = 65536
COLS = 1024
LEVELS = 2
N_GROUP = 4


def draw_snapshot_basis(key, part):
    key_scale = jax.random.fold_in(key, 11)
    key_entry = jax.random.fold_in(key, 12)
    slabs = ROWS // ROWS_DEV
    logs = jax.random.uniform(key_scale, (slabs, 1, COLS), jnp.float32, jnp.log(0.1), jnp.log(1.5))
    scales = jnp.exp(logs)
    ramp = jnp.exp(jnp.log(3.0) * jnp.arange(ROWS, dtype=jnp.float32) / ROWS)
    ramp = ramp.reshape(slabs, ROWS_DEV, 1)
    entries = jax.random.normal(key_entry, (ROWS, COLS), jnp.float32)
    base = jnp.clip(entries, -6.0, 6.0).reshape(slabs, ROWS_DEV, COLS)
    values = base * scales * ramp
    return values.reshape(ROWS, COLS).astype(jnp.bfloat16)


def normal_values(own_key, extent, deviation, bound, kind=jnp.bfloat16):
    result = deviation * jax.random.normal(own_key, extent, jnp.float32)
    return jnp.clip(result, min=-bound, max=bound).astype(kind)


def setup_inputs(seed: int = 0) -> dict:
    key_list = jax.random.split(jax.random.key(seed), 3)
    snapshot_basis = draw_snapshot_basis(jax.random.fold_in(key_list[2], 71), 0)
    sketch = normal_values(key_list[1], (LEVELS, 2 * K, K), (2 * K) ** -0.5, 0.25, jnp.float32)
    return dict(snapshot_basis=snapshot_basis, sketch=sketch)


def filter_mix(gram, sketch_level):
    width = gram.shape[0]
    eye = jnp.eye(width, dtype=jnp.float32)
    scaled = gram / (jnp.trace(gram) / width)
    shifted = scaled - eye
    iterate = shifted / (1.0 + jnp.sqrt(jnp.sum(shifted * shifted)))
    for step in range(STEPS):
        square = jnp.dot(iterate, iterate, precision=lax.Precision.HIGHEST)
        cube = jnp.dot(square, iterate, precision=lax.Precision.HIGHEST)
        iterate = 1.5 * iterate - 0.5 * cube
    applied = jnp.dot(iterate, sketch_level, precision=lax.Precision.HIGHEST)
    return (0.5 * (sketch_level + applied)).astype(jnp.bfloat16)

def merge_pair(lower, upper, sketch_level):
    stacked = jnp.concatenate([lower, upper], axis=1)
    gram = lax.dot_general(stacked, stacked, (((0,), (0,)), ((), ())), preferred_element_type=jnp.float32)
    mix = filter_mix(gram, sketch_level)
    return jnp.dot(stacked, mix, preferred_element_type=jnp.float32).astype(jnp.bfloat16)

def reference(snapshot_basis, sketch):
    panels = [snapshot_basis[:, g * K:(g + 1) * K] for g in range(N_GROUP)]
    for level in range(LEVELS):
        reach = 2 ** level
        fresh = list(panels)
        for lower in range(N_GROUP):
            if lower >> level & 1 == 0:
                merged = merge_pair(panels[lower], panels[lower + reach], sketch[level])
                fresh[lower] = merged
                fresh[lower + reach] = merged
        panels = fresh
    return panels[0]
```

```python
import functools

import jax
import jax.numpy as jnp
from jax import lax
from jax.experimental import pallas as pl
from jax.experimental.pallas import tpu as pltpu
from jax.sharding import PartitionSpec as P

STEPS = 5
F32 = jnp.float32
BF16 = jnp.bfloat16


def swap(block, axis, offset):
    count = lax.axis_size(axis)
    return lax.ppermute(block, axis, [(i, i ^ offset) for i in range(count)])


def after(value, *others):
    return lax.optimization_barrier((value,) + others)[0]


def dot_t(a, b):
    return lax.dot_general(a, b, (((0,), (0,)), ((), ())), preferred_element_type=F32)


def dot(a, b):
    return jnp.dot(a, b, preferred_element_type=F32)


def split(x):
    high = x.astype(BF16)
    return high, (x - high.astype(F32)).astype(BF16)


def dot3(a, b):
    ah, al = a
    bh, bl = b
    return dot(ah, bh) + (dot(ah, bl) + dot(al, bh))


def own_gram_kernel(ids, x_ref, *refs):
    outs, acc = refs[:-1], refs[-1]
    step = pl.program_id(0)

    @pl.when(step == 0)
    def _():
        acc[...] = jnp.zeros_like(acc)

    x = x_ref[...]
    acc[...] += dot_t(x, x)

    @pl.when(step == pl.num_programs(0) - 1)
    def _():
        write_slices(ids[0], acc, outs)


def write_slices(me, acc, outs):
    rows = outs[0].shape[0]
    for k, out in enumerate(outs):
        start = pl.multiple_of(jnp.bitwise_xor(me, k) * rows, rows)
        out[...] = acc[pl.ds(start, rows), :]


def own_gram(ids, panel, parts):
    rows, width = panel.shape
    tile = min(rows, 2048)
    shape = jax.ShapeDtypeStruct((width // parts, width), F32)
    whole = pl.BlockSpec((width // parts, width), lambda i, ids: (0, 0))
    return pl.pallas_call(
        own_gram_kernel,
        grid_spec=pltpu.PrefetchScalarGridSpec(
            num_scalar_prefetch=1,
            grid=(rows // tile,),
            in_specs=[pl.BlockSpec((tile, width), lambda i, ids: (i, 0))],
            out_specs=[whole] * parts,
            scratch_shapes=[pltpu.VMEM((width, width), F32)],
        ),
        out_shape=[shape] * parts,
        name="own_gram",
    )(ids, panel)


def cross_kernel(sliced, chained, ids, own_ref, other_ref, *refs):
    if chained:
        start, refs = refs[0], refs[1:]
    outs, acc = refs[:-1], refs[-1]
    step = pl.program_id(0)

    @pl.when(step == 0)
    def _():
        acc[...] = start[...] if chained else jnp.zeros_like(acc)

    width = acc.shape[0]
    own = own_ref[...].reshape(-1, width)
    other = other_ref[...].reshape(-1, width)

    @pl.when(ids[1] == 0)
    def _():
        acc[...] += dot_t(own, other)

    @pl.when(ids[1] == 1)
    def _():
        acc[...] += dot_t(other, own)

    @pl.when(step == pl.num_programs(0) - 1)
    def _():
        if sliced:
            write_slices(ids[0], acc, outs)
        else:
            outs[0][...] = acc[...]


def cross_gram(ids, blocks, other, where, start, parts):
    outer, _, _, block_rows, width = blocks.shape
    sliced = parts > 0
    chained = start is not None
    count = parts if sliced else 1
    shape = jax.ShapeDtypeStruct((width // count, width), F32)
    whole = pl.BlockSpec((width // count, width), lambda i, ids: (0, 0))
    in_specs = [
        pl.BlockSpec((1, 1, 1, block_rows, width), lambda i, ids: (i, ids[where], ids[1], 0, 0)),
        pl.BlockSpec((1, block_rows, width), lambda i, ids: (i, 0, 0)),
    ]
    args = [blocks, other]
    if chained:
        in_specs.append(pl.BlockSpec((width, width), lambda i, ids: (0, 0)))
        args.append(start)
    return pl.pallas_call(
        functools.partial(cross_kernel, sliced, chained),
        grid_spec=pltpu.PrefetchScalarGridSpec(
            num_scalar_prefetch=1,
            grid=(outer,),
            in_specs=in_specs,
            out_specs=[whole] * count,
            scratch_shapes=[pltpu.VMEM((width, width), F32)],
        ),
        out_shape=[shape] * count,
        name="cross_gram",
    )(ids, *args)


def assemble_kernel(ids, *refs):
    pieces, out = refs[:-1], refs[-1]
    rows = pieces[0].shape[1]
    for k, piece in enumerate(pieces):
        start = pl.multiple_of(jnp.bitwise_xor(ids[0], k) * rows, rows)
        out[:, pl.ds(start, rows), :] = piece[...]


def assemble(ids, pieces):
    lead, rows, width = pieces[0].shape
    return pl.pallas_call(
        assemble_kernel,
        in_specs=[pl.BlockSpec(memory_space=pltpu.SMEM)]
        + [pl.BlockSpec(memory_space=pltpu.VMEM)] * len(pieces),
        out_specs=pl.BlockSpec(memory_space=pltpu.VMEM),
        out_shape=jax.ShapeDtypeStruct((lead, rows * len(pieces), width), F32),
        name="assemble",
    )(ids, *pieces)


def filter_kernel(pairs, further, ids, diag, sketch, *refs):
    outs = 2 if further else 1
    pieces, refs = refs[: -(outs + 2)], refs[-(outs + 2):]
    mix_ref, gram, iterate = refs[0], refs[-2], refs[-1]
    rows, width = pieces[0].shape[1:]
    full = 2 * width
    for p in range(pairs):
        gram[p, :width, :width] = diag[2 * p]
        gram[p, width:, width:] = diag[2 * p + 1]
        for k, piece in enumerate(pieces):
            start = pl.multiple_of(jnp.bitwise_xor(ids[0], k) * rows, rows)
            gram[p, pl.ds(start, rows), width:] = piece[p]
        gram[p, width:, :width] = gram[p, :width, width:].T
    eye = lax.broadcasted_iota(jnp.int32, (full, full), 0) == lax.broadcasted_iota(
        jnp.int32, (full, full), 1
    )
    for p in range(pairs):
        whole = gram[p]
        trace = jnp.sum(jnp.where(eye, whole, 0.0), keepdims=True)
        shifted = whole / (trace / full) - jnp.where(eye, 1.0, 0.0)
        norm = jnp.sqrt(jnp.sum(shifted * shifted, keepdims=True))
        iterate[p] = shifted / (1.0 + norm)

    def step(_, carry):
        xs = [iterate[p] for p in range(pairs)]
        parts = [split(x) for x in xs]
        squares = [split(dot3(part, part)) for part in parts]
        for p in range(pairs):
            iterate[p] = 1.5 * xs[p] - 0.5 * dot3(parts[p], squares[p])
        return carry

    lax.fori_loop(0, STEPS - 1, step, 0)
    given = sketch[...]
    given_parts = split(given)
    parts = [split(iterate[p]) for p in range(pairs)]
    first = [dot3(part, given_parts) for part in parts]
    second = [dot3(part, split(t)) for part, t in zip(parts, first)]
    third = [dot3(part, split(t)) for part, t in zip(parts, second)]
    for p in range(pairs):
        applied = 1.5 * first[p] - 0.5 * third[p]
        mix = (0.5 * (given + applied)).astype(BF16)
        mix_ref[p, 0] = mix[:width]
        mix_ref[p, 1] = mix[width:]
        if further:
            gh, gl = split(gram[p])
            th, tl = split(dot(gh, mix) + dot(gl, mix))
            refs[1][p] = dot_t(mix, th) + dot_t(mix, tl)


def filter_mix(ids, diag, pieces, sketch_level, further):
    pairs, _, width = pieces[0].shape
    vmem = pl.BlockSpec(memory_space=pltpu.VMEM)
    out_shape = [jax.ShapeDtypeStruct((pairs, 2, width, width), BF16)]
    if further:
        out_shape.append(jax.ShapeDtypeStruct((pairs, width, width), F32))
    return pl.pallas_call(
        functools.partial(filter_kernel, pairs, further),
        in_specs=[pl.BlockSpec(memory_space=pltpu.SMEM)] + [vmem] * (2 + len(pieces)),
        out_specs=[vmem] * len(out_shape),
        out_shape=out_shape,
        scratch_shapes=[pltpu.VMEM((pairs, 2 * width, 2 * width), F32)] * 2,
        name="filter_mix",
    )(ids, diag, sketch_level, *pieces)


def merge_own_kernel(ids, own, other, mix, out):
    width = mix.shape[-1]
    bit0, bit1 = ids[1], ids[2]
    a = own[...].reshape(-1, width)
    b = other[...].reshape(-1, width)
    out[...] = (dot(a, mix[bit1, bit0]) + dot(b, mix[bit1, 1 - bit0])).astype(BF16)


def merge_own(ids, blocks, other, mix):
    outer, _, _, block_rows, width = blocks.shape
    tile = min(block_rows, 1024)
    cuts = block_rows // tile
    return pl.pallas_call(
        merge_own_kernel,
        grid_spec=pltpu.PrefetchScalarGridSpec(
            num_scalar_prefetch=1,
            grid=(outer, cuts),
            in_specs=[
                pl.BlockSpec(
                    (1, 1, 1, tile, width), lambda i, r, ids: (i, ids[2], ids[1], r, 0)
                ),
                pl.BlockSpec((1, tile, width), lambda i, r, ids: (i, r, 0)),
                pl.BlockSpec(mix.shape, lambda i, r, ids: (0, 0, 0, 0)),
            ],
            out_specs=pl.BlockSpec((tile, width), lambda i, r, ids: (i * cuts + r, 0)),
        ),
        out_shape=jax.ShapeDtypeStruct((outer * block_rows, width), BF16),
        name="merge_own",
    )(ids, blocks, other, mix)


def merge_other_kernel(ids, outer_panel, near, passed, own_merged, mix, *refs):
    merged, outs, acc = refs[0], refs[1:-1], refs[-1]
    step = pl.program_id(0)
    bit0, bit1 = ids[1], ids[2]
    pair = 1 - bit1

    @pl.when(step == 0)
    def _():
        acc[...] = jnp.zeros_like(acc)

    def run(inner_ref):
        fresh = dot(outer_panel[...], mix[pair, pair]) + dot(inner_ref[...], mix[pair, 1 - pair])
        merged[...] = fresh.astype(BF16)

    @pl.when(bit0 != bit1)
    def _():
        run(near)

    @pl.when(bit0 == bit1)
    def _():
        run(passed)

    @pl.when(bit1 == 0)
    def _():
        acc[...] += dot_t(own_merged[...], merged[...])

    @pl.when(bit1 == 1)
    def _():
        acc[...] += dot_t(merged[...], own_merged[...])

    @pl.when(step == pl.num_programs(0) - 1)
    def _():
        write_slices(ids[0], acc, outs)


def merge_other(ids, outer_panel, near, passed, own_merged, mix, parts):
    rows, width = own_merged.shape
    tile = min(rows, 1024)
    panel = pl.BlockSpec((tile, width), lambda i, ids: (i, 0))
    shape = jax.ShapeDtypeStruct((width // parts, width), F32)
    whole = pl.BlockSpec((width // parts, width), lambda i, ids: (0, 0))
    return pl.pallas_call(
        merge_other_kernel,
        grid_spec=pltpu.PrefetchScalarGridSpec(
            num_scalar_prefetch=1,
            grid=(rows // tile,),
            in_specs=[panel] * 4 + [pl.BlockSpec(mix.shape, lambda i, ids: (0, 0, 0, 0))],
            out_specs=[panel] + [whole] * parts,
            scratch_shapes=[pltpu.VMEM((width, width), F32)],
        ),
        out_shape=[jax.ShapeDtypeStruct((rows, width), BF16)] + [shape] * parts,
        name="merge_other",
    )(ids, outer_panel, near, passed, own_merged, mix)


def combine_kernel(ids, which, own, other, mix, out):
    bit = ids[which]
    out[...] = (dot(own[...], mix[0, bit]) + dot(other[...], mix[0, 1 - bit])).astype(BF16)


def combine(ids, which, own, other, mix):
    rows, width = own.shape
    tile = min(rows, 1024)
    panel = pl.BlockSpec((tile, width), lambda i, ids: (i, 0))
    return pl.pallas_call(
        lambda ids, *refs: combine_kernel(ids, which, *refs),
        grid_spec=pltpu.PrefetchScalarGridSpec(
            num_scalar_prefetch=1,
            grid=(rows // tile,),
            in_specs=[panel] * 2 + [pl.BlockSpec(mix.shape, lambda i, ids: (0, 0, 0, 0))],
            out_specs=panel,
        ),
        out_shape=jax.ShapeDtypeStruct((rows, width), BF16),
        name="combine",
    )(ids, own, other, mix)


def scatter_space(pieces):
    total = pieces[0]
    got = [swap(piece, "space", k) for k, piece in enumerate(pieces) if k > 0]
    for piece in got:
        total = total + piece
    return total


def gather_space(piece):
    count = lax.axis_size("space")
    pieces = [piece] + [None] * (count - 1)
    for k in range(2, count, 2):
        pieces[k] = swap(piece, "space", k)
    for k in range(0, count, 2):
        pieces[k + 1] = swap(pieces[k], "space", 1)
    return pieces


def body(snapshot_basis, sketch):
    rows, width = snapshot_basis.shape
    groups = lax.axis_size("group")
    parts = lax.axis_size("space")
    levels = groups.bit_length() - 1
    member = lax.axis_index("group")
    bit0 = member & 1
    bit1 = member >> 1 & 1
    inner = bit0 != bit1
    ids = jnp.stack([lax.axis_index("space"), bit0, bit1, 1 - bit1]).astype(jnp.int32)
    block_rows = rows // groups
    outer = groups // 4
    blocks = snapshot_basis.reshape(outer, 2, 2, block_rows, width)

    def pick(index1, index0):
        start = (0, index1, index0, 0, 0)
        cut = lax.dynamic_slice(blocks, start, (outer, 1, 1, block_rows, width))
        return cut.reshape(outer, block_rows, width)

    middle = []
    forward = []
    for base in range(0, groups, 4):
        middle += [(base + 1, base + 2), (base + 2, base + 1)]
        forward += [(base + 1, base), (base + 2, base + 3)]

    far = swap(pick(1 - bit1, 1 - bit0), "group", 1)
    inner_pass = lax.ppermute(pick(1 - bit1, bit0), "group", middle)

    own_slices = own_gram(ids, snapshot_basis, parts)
    own_sum = scatter_space(own_slices)
    turned = [swap(own_sum, "group", k) for k in (1, 2, 3)]
    order = [own_sum] + turned

    near_piece = after(pick(bit1, 1 - bit0), own_sum)
    near = swap(near_piece, "group", 1)
    inner_keep = lax.ppermute(after(pick(1 - bit1, 1 - bit0), own_sum), "group", middle)

    quad = member & 3
    stacked = jnp.stack(order)
    diag_slices = jnp.stack(
        [lax.dynamic_index_in_dim(stacked, quad ^ g, 0, keepdims=False) for g in range(4)]
    )
    diag = assemble(ids, gather_space(diag_slices))

    half = cross_gram(ids, blocks, far, 3, None, 0)[0]
    cross_slices = cross_gram(ids, blocks, near, 2, half, parts)
    cross_sum = scatter_space(cross_slices)
    one, two, three = [swap(cross_sum, "group", k) for k in (1, 2, 3)]
    mine = cross_sum + one
    theirs = two + three
    both = jnp.stack([jnp.where(bit1 == 0, mine, theirs), jnp.where(bit1 == 0, theirs, mine)])

    outer_own = jnp.where(inner, far, pick(1 - bit1, bit0))
    outer_panel = swap(after(outer_own, both), "group", 2)
    passed = lax.ppermute(after(inner_pass, both), "group", forward)

    mix, diag = filter_mix(ids, diag, gather_space(both), sketch[0], True)

    flat = lambda a: a.reshape(-1, width)
    own_merged = merge_own(ids, blocks, near, mix)
    results = merge_other(
        ids, flat(outer_panel), flat(inner_keep), flat(passed), own_merged, mix, parts
    )
    other_merged, slices = results[0], results[1:]
    total = scatter_space(slices)
    one, two, three = [swap(total, "group", k) for k in (1, 2, 3)]
    total = (total + one) + (two + three)
    more = levels > 2
    result = filter_mix(ids, diag, gather_space(total[None]), sketch[1], more)
    merged = combine(ids, 2, own_merged, other_merged, result[0])

    for level in range(2, levels):
        bit = member >> level & 1
        blocks = merged.reshape(-1, 2, block_rows, width)
        kept = flat(lax.dynamic_index_in_dim(blocks, bit, 1, keepdims=False))
        given = flat(lax.dynamic_index_in_dim(blocks, 1 - bit, 1, keepdims=False))
        got = swap(given, "group", 1 << level)
        diag_own = result[1][0]
        diag_got = swap(diag_own, "group", 1 << level)
        lower = jnp.where(bit == 0, kept, got)
        upper = jnp.where(bit == 0, got, kept)
        cross = dot_t(lower, upper).reshape(parts, width // parts, width)
        place = lax.axis_index("space")
        total = scatter_space(
            [lax.dynamic_index_in_dim(cross, place ^ k, 0, keepdims=False) for k in range(parts)]
        )
        for low in range(level + 1):
            total = total + swap(total, "group", 1 << low)
        diag = jnp.stack(
            [jnp.where(bit == 0, diag_own, diag_got), jnp.where(bit == 0, diag_got, diag_own)]
        )
        more = level + 1 < levels
        result = filter_mix(ids, diag, gather_space(total[None]), sketch[level], more)
        mix = result[0]
        merged = (dot(lower, mix[0, 0]) + dot(upper, mix[0, 1])).astype(BF16)
    return merged.reshape(block_rows, width)


def solution(mesh):
    in_specs = (P("space", "group"), P())
    out_specs = P(("space", "group"), None)
    return jax.shard_map(body, mesh=mesh, in_specs=in_specs, out_specs=out_specs, check_vma=False)
```

```python
import functools

import jax
import jax.numpy as jnp
from jax import lax
from jax.experimental import pallas as pl
from jax.experimental.pallas import tpu as pltpu
from jax.sharding import PartitionSpec as P


STEPS = 5
F32 = jnp.float32
BF16 = jnp.bfloat16


def swap(block, axis, offset):
    count = lax.axis_size(axis)
    return lax.ppermute(block, axis, [(i, i ^ offset) for i in range(count)])


def after(value, *others):
    return lax.optimization_barrier((value,) + others)[0]


def dot_t(a, b):
    return lax.dot_general(a, b, (((0,), (0,)), ((), ())), preferred_element_type=F32)


def dot(a, b):
    return jnp.dot(a, b, preferred_element_type=F32)


def split(x):
    high = x.astype(BF16)
    return high, (x - high.astype(F32)).astype(BF16)


def dot3(a, b):
    ah, al = a
    bh, bl = b
    return dot(ah, bh) + (dot(ah, bl) + dot(al, bh))


def write_slices(me, acc, outs):
    rows = outs[0].shape[0]
    for k, out in enumerate(outs):
        start = pl.multiple_of(jnp.bitwise_xor(me, k) * rows, rows)
        out[...] = acc[pl.ds(start, rows), :]


def own_gram_kernel(ids, x_ref, *refs):
    outs, acc = refs[:-1], refs[-1]
    step = pl.program_id(0)

    @pl.when(step == 0)
    def _():
        acc[...] = jnp.zeros_like(acc)

    x = x_ref[...]
    acc[...] += dot_t(x, x)

    @pl.when(step == pl.num_programs(0) - 1)
    def _():
        write_slices(ids[0], acc, outs)


def own_gram(ids, panel, parts):
    rows, width = panel.shape
    tile = rows // 8
    shape = jax.ShapeDtypeStruct((width // parts, width), F32)
    whole = pl.BlockSpec((width // parts, width), lambda i, ids: (0, 0))
    return pl.pallas_call(
        own_gram_kernel,
        grid_spec=pltpu.PrefetchScalarGridSpec(
            num_scalar_prefetch=1,
            grid=(rows // tile,),
            in_specs=[pl.BlockSpec((tile, width), lambda i, ids: (i, 0))],
            out_specs=[whole] * parts,
            scratch_shapes=[pltpu.VMEM((width, width), F32)],
        ),
        out_shape=[shape] * parts,
        name="own_gram",
    )(ids, panel)


def first_step():
    return (pl.program_id(0) == 0) & (pl.program_id(1) == 0)


def last_step():
    return (pl.program_id(0) == pl.num_programs(0) - 1) & (
        pl.program_id(1) == pl.num_programs(1) - 1
    )


def cross_kernel(sliced, chained, ids, own_ref, other_ref, *refs):
    if chained:
        start, refs = refs[0], refs[1:]
    outs, acc = refs[:-1], refs[-1]

    @pl.when(first_step())
    def _():
        acc[...] = start[...] if chained else jnp.zeros_like(acc)

    width = acc.shape[0]
    own = own_ref[...].reshape(-1, width)
    other = other_ref[...].reshape(-1, width)

    @pl.when(ids[1] == 0)
    def _():
        acc[...] += dot_t(own, other)

    @pl.when(ids[1] == 1)
    def _():
        acc[...] += dot_t(other, own)

    @pl.when(last_step())
    def _():
        if sliced:
            write_slices(ids[0], acc, outs)
        else:
            outs[0][...] = acc[...]


def cross_gram(ids, blocks, other, begin, where, start, parts):
    outer, rows, width = other.shape
    tile = min(rows, blocks.shape[3] // 4)
    shift = begin // tile
    sliced = parts > 0
    chained = start is not None
    count = parts if sliced else 1
    shape = jax.ShapeDtypeStruct((width // count, width), F32)
    whole = pl.BlockSpec((width // count, width), lambda i, r, ids: (0, 0))
    in_specs = [
        pl.BlockSpec(
            (1, 1, 1, tile, width), lambda i, r, ids: (i, ids[where], ids[1], shift + r, 0)
        ),
        pl.BlockSpec((1, tile, width), lambda i, r, ids: (i, r, 0)),
    ]
    args = [blocks, other]
    if chained:
        in_specs.append(pl.BlockSpec((width, width), lambda i, r, ids: (0, 0)))
        args.append(start)
    return pl.pallas_call(
        functools.partial(cross_kernel, sliced, chained),
        grid_spec=pltpu.PrefetchScalarGridSpec(
            num_scalar_prefetch=1,
            grid=(outer, rows // tile),
            in_specs=in_specs,
            out_specs=[whole] * count,
            scratch_shapes=[pltpu.VMEM((width, width), F32)],
        ),
        out_shape=[shape] * count,
        name="cross_gram",
    )(ids, *args)


def assemble_kernel(ids, *refs):
    pieces, out = refs[:-1], refs[-1]
    rows = pieces[0].shape[1]
    for k, piece in enumerate(pieces):
        start = pl.multiple_of(jnp.bitwise_xor(ids[0], k) * rows, rows)
        out[:, pl.ds(start, rows), :] = piece[...]


def assemble(ids, pieces):
    lead, rows, width = pieces[0].shape
    return pl.pallas_call(
        assemble_kernel,
        in_specs=[pl.BlockSpec(memory_space=pltpu.SMEM)]
        + [pl.BlockSpec(memory_space=pltpu.VMEM)] * len(pieces),
        out_specs=pl.BlockSpec(memory_space=pltpu.VMEM),
        out_shape=jax.ShapeDtypeStruct((lead, rows * len(pieces), width), F32),
        name="assemble",
    )(ids, *pieces)


def run_filter(pairs, ids, diag, sketch, pieces, gram, iterate):
    rows, width = pieces[0].shape[1:]
    full = 2 * width
    for p in range(pairs):
        gram[p, :width, :width] = diag[2 * p]
        gram[p, width:, width:] = diag[2 * p + 1]
        for k, piece in enumerate(pieces):
            start = pl.multiple_of(jnp.bitwise_xor(ids[0], k) * rows, rows)
            gram[p, pl.ds(start, rows), width:] = piece[p]
        gram[p, width:, :width] = gram[p, :width, width:].T
    eye = lax.broadcasted_iota(jnp.int32, (full, full), 0) == lax.broadcasted_iota(
        jnp.int32, (full, full), 1
    )
    for p in range(pairs):
        whole = gram[p]
        trace = jnp.sum(jnp.where(eye, whole, 0.0), keepdims=True)
        shifted = whole / (trace / full) - jnp.where(eye, 1.0, 0.0)
        norm = jnp.sqrt(jnp.sum(shifted * shifted, keepdims=True))
        iterate[p] = shifted / (1.0 + norm)

    def step(_, carry):
        xs = [iterate[p] for p in range(pairs)]
        short = [x.astype(BF16) for x in xs]
        squares = [dot(x, x).astype(BF16) for x in short]
        for p in range(pairs):
            iterate[p] = 1.5 * xs[p] - 0.5 * dot(short[p], squares[p])
        return carry

    lax.fori_loop(0, STEPS - 1, step, 0)
    given = sketch[...]
    given_parts = split(given)
    parts = [split(iterate[p]) for p in range(pairs)]
    first = [dot3(part, given_parts) for part in parts]
    second = [dot3(part, split(t)) for part, t in zip(parts, first)]
    third = [dot3(part, split(t)) for part, t in zip(parts, second)]
    mixes = []
    for p in range(pairs):
        applied = 1.5 * first[p] - 0.5 * third[p]
        mixes.append((0.5 * (given + applied)).astype(BF16))
    return mixes


def next_diag(gram, mix):
    gh, gl = split(gram)
    th, tl = split(dot(gh, mix) + dot(gl, mix))
    return dot_t(mix, th) + dot_t(mix, tl)


def pair_filter_kernel(ids, diag, sketch, *refs):
    pieces, (mix_ref, diag_ref, gram, iterate) = refs[:-4], refs[-4:]
    width = diag.shape[-1]
    mixes = run_filter(2, ids, diag, sketch, pieces, gram, iterate)
    for p in range(2):
        mix_ref[p, 0] = mixes[p][:width]
        mix_ref[p, 1] = mixes[p][width:]
        diag_ref[p] = next_diag(gram[p], mixes[p])


def pair_filter(ids, diag, pieces, sketch_level):
    pairs, _, width = pieces[0].shape
    vmem = pl.BlockSpec(memory_space=pltpu.VMEM)
    return pl.pallas_call(
        pair_filter_kernel,
        in_specs=[pl.BlockSpec(memory_space=pltpu.SMEM)] + [vmem] * (2 + len(pieces)),
        out_specs=[vmem] * 2,
        out_shape=[
            jax.ShapeDtypeStruct((pairs, 2, width, width), BF16),
            jax.ShapeDtypeStruct((pairs, width, width), F32),
        ],
        scratch_shapes=[pltpu.VMEM((pairs, 2 * width, 2 * width), F32)] * 2,
        name="pair_filter",
    )(ids, diag, sketch_level, *pieces)


def merge_filter_kernel(which, cuts, ids, diag, sketch, *refs):
    own, others = refs[0], refs[1 : 1 + cuts]
    pieces, (out, diag_ref, mix_ref, gram, iterate) = refs[1 + cuts : -5], refs[-5:]
    width = diag.shape[-1]
    mix = run_filter(1, ids, diag, sketch, pieces, gram, iterate)[0]
    mix_ref[0] = mix[:width]
    mix_ref[1] = mix[width:]
    bit = ids[which]
    begin = 0
    for other in others:
        rows = other.shape[1]
        for h in range(other.shape[0]):
            here = slice(begin, begin + rows)
            total = dot(own[h, here], mix_ref[bit]) + dot(other[h], mix_ref[1 - bit])
            out[h, here] = total.astype(BF16)
        begin += rows
    diag_ref[...] = next_diag(gram[0], mix)


def merge_filter(ids, diag, pieces, sketch_level, which, own, others):
    _, _, width = pieces[0].shape
    vmem = pl.BlockSpec(memory_space=pltpu.VMEM)
    return pl.pallas_call(
        functools.partial(merge_filter_kernel, which, len(others)),
        in_specs=[pl.BlockSpec(memory_space=pltpu.SMEM)]
        + [vmem] * (3 + len(others) + len(pieces)),
        out_specs=[vmem] * 2,
        out_shape=[
            jax.ShapeDtypeStruct(own.shape, BF16),
            jax.ShapeDtypeStruct((width, width), F32),
        ],
        scratch_shapes=[pltpu.VMEM((2, width, width), BF16)]
        + [pltpu.VMEM((1, 2 * width, 2 * width), F32)] * 2,
        name="merge_filter",
    )(ids, diag, sketch_level, own, *others, *pieces)


def merge_own_kernel(ids, own, other, mix, out):
    width = mix.shape[-1]
    bit0, bit1 = ids[1], ids[2]
    a = own[...].reshape(-1, width)
    b = other[...].reshape(-1, width)
    fresh = dot(a, mix[bit1, bit0]) + dot(b, mix[bit1, 1 - bit0])
    out[...] = fresh.astype(BF16).reshape(out.shape)


def merge_own(ids, blocks, other, begin, mix):
    outer, rows, width = other.shape
    tile = min(rows, blocks.shape[3] // 4)
    shift = begin // tile
    part = pl.BlockSpec((1, tile, width), lambda i, r, ids: (i, r, 0))
    return pl.pallas_call(
        merge_own_kernel,
        grid_spec=pltpu.PrefetchScalarGridSpec(
            num_scalar_prefetch=1,
            grid=(outer, rows // tile),
            in_specs=[
                pl.BlockSpec(
                    (1, 1, 1, tile, width), lambda i, r, ids: (i, ids[2], ids[1], shift + r, 0)
                ),
                part,
                pl.BlockSpec(mix.shape, lambda i, r, ids: (0, 0, 0, 0)),
            ],
            out_specs=part,
        ),
        out_shape=jax.ShapeDtypeStruct((outer, rows, width), BF16),
        name="merge_own",
    )(ids, blocks, other, mix)


def merge_other_kernel(chained, ids, out_near, in_near, out_far, in_far, own_merged, mix, *refs):
    if chained:
        start, refs = refs[0], refs[1:]
    merged, outs, acc = refs[0], refs[1:-1], refs[-1]
    bit0, bit1 = ids[1], ids[2]
    pair = 1 - bit1

    @pl.when(first_step())
    def _():
        acc[...] = start[...] if chained else jnp.zeros_like(acc)

    def run(outer_ref, inner_ref):
        fresh = dot(outer_ref[0], mix[pair, pair]) + dot(inner_ref[0], mix[pair, 1 - pair])
        merged[0] = fresh.astype(BF16)

    @pl.when(bit0 != bit1)
    def _():
        run(out_near, in_near)

    @pl.when(bit0 == bit1)
    def _():
        run(out_far, in_far)

    @pl.when(bit1 == 0)
    def _():
        acc[...] += dot_t(own_merged[0], merged[0])

    @pl.when(bit1 == 1)
    def _():
        acc[...] += dot_t(merged[0], own_merged[0])

    @pl.when(last_step())
    def _():
        if len(outs) == 1:
            outs[0][...] = acc[...]
        else:
            write_slices(ids[0], acc, outs)


def merge_other(ids, panels, begins, sizes, own_begin, own_merged, mix, start, parts):
    outer, _, width = own_merged.shape
    rows = sizes
    tile = rows
    while any(b % tile for b in begins + [own_begin]) or tile > 512:
        tile //= 2
    shifts = [b // tile for b in begins + [own_begin]]
    specs = [
        pl.BlockSpec((1, tile, width), functools.partial(lambda s, i, r, ids: (i, s + r, 0), s))
        for s in shifts
    ]
    count = max(parts, 1)
    shape = jax.ShapeDtypeStruct((width // count, width), F32)
    whole = pl.BlockSpec((width // count, width), lambda i, r, ids: (0, 0))
    chained = start is not None
    more = [pl.BlockSpec((width, width), lambda i, r, ids: (0, 0))] if chained else []
    return pl.pallas_call(
        functools.partial(merge_other_kernel, chained),
        grid_spec=pltpu.PrefetchScalarGridSpec(
            num_scalar_prefetch=1,
            grid=(outer, rows // tile),
            in_specs=specs + [pl.BlockSpec(mix.shape, lambda i, r, ids: (0, 0, 0, 0))] + more,
            out_specs=[pl.BlockSpec((1, tile, width), lambda i, r, ids: (i, r, 0))]
            + [whole] * count,
            scratch_shapes=[pltpu.VMEM((width, width), F32)],
        ),
        out_shape=[jax.ShapeDtypeStruct((outer, rows, width), BF16)] + [shape] * count,
        name="merge_other",
    )(ids, *panels, own_merged, mix, *([start] if chained else []))


def scatter_space(pieces):
    total = pieces[0]
    got = [swap(piece, "space", k) for k, piece in enumerate(pieces) if k > 0]
    for piece in got:
        total = total + piece
    return total


def gather_space(piece):
    count = lax.axis_size("space")
    pieces = [piece] + [None] * (count - 1)
    for k in range(2, count, 2):
        pieces[k] = swap(piece, "space", k)
    for k in range(0, count, 2):
        pieces[k + 1] = swap(pieces[k], "space", 1)
    return pieces


def compute(snapshot_basis, sketch):
    rows, width = snapshot_basis.shape
    groups = lax.axis_size("group")
    parts = lax.axis_size("space")
    levels = groups.bit_length() - 1
    member = lax.axis_index("group")
    bit0 = member & 1
    bit1 = member >> 1 & 1
    ids = jnp.stack([lax.axis_index("space"), bit0, bit1, 1 - bit1]).astype(jnp.int32)
    block_rows = rows // groups
    outer = groups // 4
    blocks = snapshot_basis.reshape(outer, 2, 2, block_rows, width)
    cut = block_rows * 3 // 4
    tail = block_rows - cut

    def pick(index1, index0, begin=0, size=block_rows):
        start = (0, index1, index0, begin, 0)
        return lax.dynamic_slice(blocks, start, (outer, 1, 1, size, width)).reshape(
            outer, size, width
        )

    def send(value, routes):
        return lax.ppermute(value, "group", routes)

    middle, forward, rise, leave = [], [], [], []
    for base in range(0, groups, 4):
        middle += [(base + 1, base + 2), (base + 2, base + 1)]
        forward += [(base + 1, base), (base + 2, base + 3)]
        rise += [(base + 1, base + 3), (base + 2, base)]
        leave += [(base, base + 2), (base + 3, base + 1)]
    pair = [(i, i ^ 1) for i in range(groups)]

    far = send(pick(1 - bit1, 1 - bit0), pair)
    pass_on = send(pick(1 - bit1, bit0), middle)

    own_sum = scatter_space(own_gram(ids, snapshot_basis, parts))
    turned = [own_sum] + [swap(own_sum, "group", k) for k in (1, 2, 3)]

    near_head = send(after(pick(bit1, 1 - bit0, 0, cut), own_sum), pair)
    keep = send(after(pick(1 - bit1, 1 - bit0), own_sum), middle)
    near_tail = send(after(pick(bit1, 1 - bit0, cut, tail), own_sum), pair)
    head_rise = send(after(far[:, :cut], own_sum), rise)

    quad = member & 3
    stacked = jnp.stack(turned)
    diag_slices = jnp.stack(
        [lax.dynamic_index_in_dim(stacked, quad ^ g, 0, keepdims=False) for g in range(4)]
    )
    diag = assemble(ids, gather_space(diag_slices))

    half = cross_gram(ids, blocks, far, 0, 3, None, 0)[0]
    half = cross_gram(ids, blocks, near_head, 0, 2, after(half, diag), 0)[0]
    cross_slices = cross_gram(ids, blocks, near_tail, cut, 2, half, parts)
    cross_sum = scatter_space(cross_slices)
    one, two, three = [swap(cross_sum, "group", k) for k in (1, 2, 3)]
    mine = cross_sum + one
    theirs = two + three
    both = jnp.stack([jnp.where(bit1 == 0, mine, theirs), jnp.where(bit1 == 0, theirs, mine)])

    head_leave = send(after(pick(1 - bit1, bit0, 0, cut), both), leave)
    head_pass = send(after(pass_on[:, :cut], both), forward)
    tail_rise = send(after(far[:, cut:], both), rise)
    tail_leave = send(after(pick(1 - bit1, bit0, cut, tail), both), leave)
    tail_pass = send(after(pass_on[:, cut:], both), forward)

    mix, diag = pair_filter(ids, diag, gather_space(both), sketch[0])

    own_head = merge_own(ids, blocks, near_head, 0, mix)
    own_tail = merge_own(ids, blocks, near_tail, cut, mix)
    other_head, half = merge_other(
        ids, [head_leave, keep, head_rise, head_pass], [0] * 4, cut, 0, own_head, mix, None, 0
    )
    results = merge_other(
        ids, [tail_leave, keep, tail_rise, tail_pass], [0, cut, 0, 0], tail, 0, own_tail, mix,
        half, parts,
    )
    other_tail, slices = results[0], results[1:]
    total = scatter_space(slices)
    one, two, three = [swap(total, "group", k) for k in (1, 2, 3)]
    total = (total + one) + (two + three)
    own_merged = jnp.concatenate([own_head, own_tail], axis=1)
    merged, diag_own = merge_filter(
        ids, diag, gather_space(total[None]), sketch[1], 2, own_merged, [other_head, other_tail]
    )

    for level in range(2, levels):
        bit = member >> level & 1
        pairs = merged.reshape(-1, 2, block_rows, width)
        kept = lax.dynamic_index_in_dim(pairs, bit, 1, keepdims=False)
        given = lax.dynamic_index_in_dim(pairs, 1 - bit, 1, keepdims=False)
        got = swap(given, "group", 1 << level)
        diag_got = swap(diag_own, "group", 1 << level)
        lower = jnp.where(bit == 0, kept, got).reshape(-1, width)
        upper = jnp.where(bit == 0, got, kept).reshape(-1, width)
        cross = dot_t(lower, upper).reshape(parts, width // parts, width)
        place = lax.axis_index("space")
        total = scatter_space(
            [lax.dynamic_index_in_dim(cross, place ^ k, 0, keepdims=False) for k in range(parts)],
        )
        for low in range(level + 1):
            total = total + swap(total, "group", 1 << low)
        diag = jnp.stack(
            [jnp.where(bit == 0, diag_own, diag_got), jnp.where(bit == 0, diag_got, diag_own)]
        )
        flag = jnp.stack([lax.axis_index("space"), bit]).astype(jnp.int32)
        merged, diag_own = merge_filter(
            flag, diag, gather_space(total[None]), sketch[level], 1, kept, [got]
        )
    return merged.reshape(block_rows, width)


def solution(mesh):
    in_specs = (P("space", "group"), P())
    out_specs = P(("space", "group"), None)
    return jax.shard_map(compute, mesh=mesh, in_specs=in_specs, out_specs=out_specs, check_vma=False)
```

```python
import functools

import jax
import jax.numpy as jnp
from jax import lax
from jax.experimental import pallas as pl
from jax.experimental.pallas import tpu as pltpu
from jax.sharding import PartitionSpec as P


STEPS = 5
F32 = jnp.float32
BF16 = jnp.bfloat16


def swap(block, axis, offset):
    count = lax.axis_size(axis)
    return lax.ppermute(block, axis, [(i, i ^ offset) for i in range(count)])


def after(value, *others):
    return lax.optimization_barrier((value,) + others)[0]


def dot_t(a, b):
    return lax.dot_general(a, b, (((0,), (0,)), ((), ())), preferred_element_type=F32)


def dot(a, b):
    return jnp.dot(a, b, preferred_element_type=F32)


def split(x):
    high = x.astype(BF16)
    return high, (x - high.astype(F32)).astype(BF16)


def dot3(a, b):
    ah, al = a
    bh, bl = b
    return dot(ah, bh) + (dot(ah, bl) + dot(al, bh))


def vmem_limit(mib):
    return pltpu.CompilerParams(vmem_limit_bytes=mib * 2**20)


def write_slices(me, acc, outs):
    rows = outs[0].shape[0]
    for k, out in enumerate(outs):
        start = pl.multiple_of(jnp.bitwise_xor(me, k) * rows, rows)
        out[...] = acc[pl.ds(start, rows), :]


def own_gram_kernel(ids, x_ref, *refs):
    outs, acc = refs[:-1], refs[-1]
    step = pl.program_id(0)

    @pl.when(step == 0)
    def _():
        acc[...] = jnp.zeros_like(acc)

    x = x_ref[...]
    acc[...] += dot_t(x, x)

    @pl.when(step == pl.num_programs(0) - 1)
    def _():
        write_slices(ids[0], acc, outs)


def own_gram(ids, panel, parts):
    rows, width = panel.shape
    tile = rows // 4
    shape = jax.ShapeDtypeStruct((width // parts, width), F32)
    whole = pl.BlockSpec((width // parts, width), lambda i, ids: (0, 0))
    return pl.pallas_call(
        own_gram_kernel,
        grid_spec=pltpu.PrefetchScalarGridSpec(
            num_scalar_prefetch=1,
            grid=(rows // tile,),
            in_specs=[pl.BlockSpec((tile, width), lambda i, ids: (i, 0))],
            out_specs=[whole] * parts,
            scratch_shapes=[pltpu.VMEM((width, width), F32)],
        ),
        out_shape=[shape] * parts,
        compiler_params=vmem_limit(8),
        name="own_gram",
    )(ids, panel)


def first_step():
    return (pl.program_id(0) == 0) & (pl.program_id(1) == 0)


def last_step():
    return (pl.program_id(0) == pl.num_programs(0) - 1) & (
        pl.program_id(1) == pl.num_programs(1) - 1
    )


def cross_kernel(sliced, chained, ids, own_ref, other_ref, *refs):
    if chained:
        start, refs = refs[0], refs[1:]
    outs, acc = refs[:-1], refs[-1]

    @pl.when(first_step())
    def _():
        acc[...] = start[...] if chained else jnp.zeros_like(acc)

    width = acc.shape[0]
    own = own_ref[...].reshape(-1, width)
    other = other_ref[...].reshape(-1, width)

    @pl.when(ids[1] == 0)
    def _():
        acc[...] += dot_t(own, other)

    @pl.when(ids[1] == 1)
    def _():
        acc[...] += dot_t(other, own)

    @pl.when(last_step())
    def _():
        if sliced:
            write_slices(ids[0], acc, outs)
        else:
            outs[0][...] = acc[...]


def cross_gram(ids, blocks, other, begin, where, start, parts):
    outer, rows, width = other.shape
    tile = min(rows, blocks.shape[3] // 4)
    shift = begin // tile
    sliced = parts > 0
    chained = start is not None
    count = parts if sliced else 1
    shape = jax.ShapeDtypeStruct((width // count, width), F32)
    whole = pl.BlockSpec((width // count, width), lambda i, r, ids: (0, 0))
    in_specs = [
        pl.BlockSpec(
            (1, 1, 1, tile, width), lambda i, r, ids: (i, ids[where], ids[1], shift + r, 0)
        ),
        pl.BlockSpec((1, tile, width), lambda i, r, ids: (i, r, 0)),
    ]
    args = [blocks, other]
    if chained:
        in_specs.append(pl.BlockSpec((width, width), lambda i, r, ids: (0, 0)))
        args.append(start)
    return pl.pallas_call(
        functools.partial(cross_kernel, sliced, chained),
        grid_spec=pltpu.PrefetchScalarGridSpec(
            num_scalar_prefetch=1,
            grid=(outer, rows // tile),
            in_specs=in_specs,
            out_specs=[whole] * count,
            scratch_shapes=[pltpu.VMEM((width, width), F32)],
        ),
        out_shape=[shape] * count,
        compiler_params=vmem_limit(8),
        name="cross_gram",
    )(ids, *args)


def assemble_kernel(ids, *refs):
    pieces, out = refs[:-1], refs[-1]
    rows = pieces[0].shape[1]
    for k, piece in enumerate(pieces):
        start = pl.multiple_of(jnp.bitwise_xor(ids[0], k) * rows, rows)
        out[:, pl.ds(start, rows), :] = piece[...]


def assemble(ids, pieces):
    lead, rows, width = pieces[0].shape
    return pl.pallas_call(
        assemble_kernel,
        in_specs=[pl.BlockSpec(memory_space=pltpu.SMEM)]
        + [pl.BlockSpec(memory_space=pltpu.VMEM)] * len(pieces),
        out_specs=pl.BlockSpec(memory_space=pltpu.VMEM),
        out_shape=jax.ShapeDtypeStruct((lead, rows * len(pieces), width), F32),
        compiler_params=vmem_limit(4),
        name="assemble",
    )(ids, *pieces)


def run_filter(pairs, ids, diag, sketch, pieces, gram, iterate):
    rows, width = pieces[0].shape[1:]
    full = 2 * width
    for p in range(pairs):
        gram[p, :width, :width] = diag[2 * p]
        gram[p, width:, width:] = diag[2 * p + 1]
        for k, piece in enumerate(pieces):
            start = pl.multiple_of(jnp.bitwise_xor(ids[0], k) * rows, rows)
            gram[p, pl.ds(start, rows), width:] = piece[p]
        gram[p, width:, :width] = gram[p, :width, width:].T
    eye = lax.broadcasted_iota(jnp.int32, (full, full), 0) == lax.broadcasted_iota(
        jnp.int32, (full, full), 1
    )
    for p in range(pairs):
        whole = gram[p]
        trace = jnp.sum(jnp.where(eye, whole, 0.0), keepdims=True)
        shifted = whole / (trace / full) - jnp.where(eye, 1.0, 0.0)
        norm = jnp.sqrt(jnp.sum(shifted * shifted, keepdims=True))
        iterate[p] = shifted / (1.0 + norm)

    def step(_, carry):
        xs = [iterate[p] for p in range(pairs)]
        short = [x.astype(BF16) for x in xs]
        squares = [dot(x, x).astype(BF16) for x in short]
        for p in range(pairs):
            iterate[p] = 1.5 * xs[p] - 0.5 * dot(short[p], squares[p])
        return carry

    lax.fori_loop(0, STEPS - 1, step, 0)
    given = sketch[...]
    given_parts = split(given)
    parts = [split(iterate[p]) for p in range(pairs)]
    first = [dot3(part, given_parts) for part in parts]
    second = [dot3(part, split(t)) for part, t in zip(parts, first)]
    third = [dot3(part, split(t)) for part, t in zip(parts, second)]
    mixes = []
    for p in range(pairs):
        applied = 1.5 * first[p] - 0.5 * third[p]
        mixes.append((0.5 * (given + applied)).astype(BF16))
    return mixes


def next_diag(gram, mix):
    gh, gl = split(gram)
    th, tl = split(dot(gh, mix) + dot(gl, mix))
    return dot_t(mix, th) + dot_t(mix, tl)


def pair_filter_kernel(ids, diag, sketch, *refs):
    pieces, (mix_ref, diag_ref, gram, iterate) = refs[:-4], refs[-4:]
    width = diag.shape[-1]
    mixes = run_filter(2, ids, diag, sketch, pieces, gram, iterate)
    for p in range(2):
        mix_ref[p, 0] = mixes[p][:width]
        mix_ref[p, 1] = mixes[p][width:]
        diag_ref[p] = next_diag(gram[p], mixes[p])


def pair_filter(ids, diag, pieces, sketch_level):
    pairs, _, width = pieces[0].shape
    vmem = pl.BlockSpec(memory_space=pltpu.VMEM)
    return pl.pallas_call(
        pair_filter_kernel,
        in_specs=[pl.BlockSpec(memory_space=pltpu.SMEM)] + [vmem] * (2 + len(pieces)),
        out_specs=[vmem] * 2,
        out_shape=[
            jax.ShapeDtypeStruct((pairs, 2, width, width), BF16),
            jax.ShapeDtypeStruct((pairs, width, width), F32),
        ],
        scratch_shapes=[pltpu.VMEM((pairs, 2 * width, 2 * width), F32)] * 2,
        compiler_params=vmem_limit(24),
        name="pair_filter",
    )(ids, diag, sketch_level, *pieces)


def merge_filter_kernel(which, cuts, ids, diag, sketch, *refs):
    own, others = refs[0], refs[1 : 1 + cuts]
    pieces, (out, diag_ref, mix_ref, gram, iterate) = refs[1 + cuts : -5], refs[-5:]
    width = diag.shape[-1]
    mix = run_filter(1, ids, diag, sketch, pieces, gram, iterate)[0]
    mix_ref[0] = mix[:width]
    mix_ref[1] = mix[width:]
    bit = ids[which]
    begin = 0
    for other in others:
        rows = other.shape[1]
        for h in range(other.shape[0]):
            here = slice(begin, begin + rows)
            total = dot(own[h, here], mix_ref[bit]) + dot(other[h], mix_ref[1 - bit])
            out[h, here] = total.astype(BF16)
        begin += rows
    diag_ref[...] = next_diag(gram[0], mix)


def merge_filter(ids, diag, pieces, sketch_level, which, own, others):
    _, _, width = pieces[0].shape
    vmem = pl.BlockSpec(memory_space=pltpu.VMEM)
    return pl.pallas_call(
        functools.partial(merge_filter_kernel, which, len(others)),
        in_specs=[pl.BlockSpec(memory_space=pltpu.SMEM)]
        + [vmem] * (3 + len(others) + len(pieces)),
        out_specs=[vmem] * 2,
        out_shape=[
            jax.ShapeDtypeStruct(own.shape, BF16),
            jax.ShapeDtypeStruct((width, width), F32),
        ],
        scratch_shapes=[pltpu.VMEM((2, width, width), BF16)]
        + [pltpu.VMEM((1, 2 * width, 2 * width), F32)] * 2,
        compiler_params=vmem_limit(24),
        name="merge_filter",
    )(ids, diag, sketch_level, own, *others, *pieces)


def merge_own_kernel(ids, own, other, mix, out):
    width = mix.shape[-1]
    bit0, bit1 = ids[1], ids[2]
    a = own[...].reshape(-1, width)
    b = other[...].reshape(-1, width)
    fresh = dot(a, mix[bit1, bit0]) + dot(b, mix[bit1, 1 - bit0])
    out[...] = fresh.astype(BF16).reshape(out.shape)


def merge_own(ids, blocks, other, begin, mix):
    outer, rows, width = other.shape
    tile = min(rows, blocks.shape[3] // 4)
    shift = begin // tile
    part = pl.BlockSpec((1, tile, width), lambda i, r, ids: (i, r, 0))
    return pl.pallas_call(
        merge_own_kernel,
        grid_spec=pltpu.PrefetchScalarGridSpec(
            num_scalar_prefetch=1,
            grid=(outer, rows // tile),
            in_specs=[
                pl.BlockSpec(
                    (1, 1, 1, tile, width), lambda i, r, ids: (i, ids[2], ids[1], shift + r, 0)
                ),
                part,
                pl.BlockSpec(mix.shape, lambda i, r, ids: (0, 0, 0, 0)),
            ],
            out_specs=part,
        ),
        out_shape=jax.ShapeDtypeStruct((outer, rows, width), BF16),
        compiler_params=vmem_limit(8),
        name="merge_own",
    )(ids, blocks, other, mix)


def merge_other_kernel(chained, ids, out_near, in_near, out_far, in_far, own_merged, mix, *refs):
    if chained:
        start, refs = refs[0], refs[1:]
    merged, outs, acc = refs[0], refs[1:-1], refs[-1]
    bit0, bit1 = ids[1], ids[2]
    pair = 1 - bit1

    @pl.when(first_step())
    def _():
        acc[...] = start[...] if chained else jnp.zeros_like(acc)

    def run(outer_ref, inner_ref):
        fresh = dot(outer_ref[0], mix[pair, pair]) + dot(inner_ref[0], mix[pair, 1 - pair])
        merged[0] = fresh.astype(BF16)

    @pl.when(bit0 != bit1)
    def _():
        run(out_near, in_near)

    @pl.when(bit0 == bit1)
    def _():
        run(out_far, in_far)

    @pl.when(bit1 == 0)
    def _():
        acc[...] += dot_t(own_merged[0], merged[0])

    @pl.when(bit1 == 1)
    def _():
        acc[...] += dot_t(merged[0], own_merged[0])

    @pl.when(last_step())
    def _():
        if len(outs) == 1:
            outs[0][...] = acc[...]
        else:
            write_slices(ids[0], acc, outs)


def merge_other(ids, panels, begins, sizes, own_begin, own_merged, mix, start, parts):
    outer, _, width = own_merged.shape
    rows = sizes
    tile = rows
    while any(b % tile for b in begins + [own_begin]) or tile > 512:
        tile //= 2
    shifts = [b // tile for b in begins + [own_begin]]
    specs = [
        pl.BlockSpec((1, tile, width), functools.partial(lambda s, i, r, ids: (i, s + r, 0), s))
        for s in shifts
    ]
    count = max(parts, 1)
    shape = jax.ShapeDtypeStruct((width // count, width), F32)
    whole = pl.BlockSpec((width // count, width), lambda i, r, ids: (0, 0))
    chained = start is not None
    more = [pl.BlockSpec((width, width), lambda i, r, ids: (0, 0))] if chained else []
    return pl.pallas_call(
        functools.partial(merge_other_kernel, chained),
        grid_spec=pltpu.PrefetchScalarGridSpec(
            num_scalar_prefetch=1,
            grid=(outer, rows // tile),
            in_specs=specs + [pl.BlockSpec(mix.shape, lambda i, r, ids: (0, 0, 0, 0))] + more,
            out_specs=[pl.BlockSpec((1, tile, width), lambda i, r, ids: (i, r, 0))]
            + [whole] * count,
            scratch_shapes=[pltpu.VMEM((width, width), F32)],
        ),
        out_shape=[jax.ShapeDtypeStruct((outer, rows, width), BF16)] + [shape] * count,
        compiler_params=vmem_limit(8),
        name="merge_other",
    )(ids, *panels, own_merged, mix, *([start] if chained else []))


def scatter_space(pieces):
    total = pieces[0]
    got = [swap(piece, "space", k) for k, piece in enumerate(pieces) if k > 0]
    for piece in got:
        total = total + piece
    return total


def gather_space(piece):
    count = lax.axis_size("space")
    pieces = [piece] + [None] * (count - 1)
    for k in range(2, count, 2):
        pieces[k] = swap(piece, "space", k)
    for k in range(0, count, 2):
        pieces[k + 1] = swap(pieces[k], "space", 1)
    return pieces


def compute(snapshot_basis, sketch):
    rows, width = snapshot_basis.shape
    groups = lax.axis_size("group")
    parts = lax.axis_size("space")
    levels = groups.bit_length() - 1
    member = lax.axis_index("group")
    bit0 = member & 1
    bit1 = member >> 1 & 1
    ids = jnp.stack([lax.axis_index("space"), bit0, bit1, 1 - bit1]).astype(jnp.int32)
    block_rows = rows // groups
    outer = groups // 4
    blocks = snapshot_basis.reshape(outer, 2, 2, block_rows, width)
    cut = block_rows * 3 // 4
    tail = block_rows - cut

    def pick(index1, index0, begin=0, size=block_rows):
        start = (0, index1, index0, begin, 0)
        return lax.dynamic_slice(blocks, start, (outer, 1, 1, size, width)).reshape(
            outer, size, width
        )

    def send(value, routes):
        return lax.ppermute(value, "group", routes)

    middle, forward, rise, leave = [], [], [], []
    for base in range(0, groups, 4):
        middle += [(base + 1, base + 2), (base + 2, base + 1)]
        forward += [(base + 1, base), (base + 2, base + 3)]
        rise += [(base + 1, base + 3), (base + 2, base)]
        leave += [(base, base + 2), (base + 3, base + 1)]
    pair = [(i, i ^ 1) for i in range(groups)]

    far = send(pick(1 - bit1, 1 - bit0), pair)
    pass_on = send(pick(1 - bit1, bit0), middle)

    own_sum = scatter_space(own_gram(ids, snapshot_basis, parts))
    turned = [own_sum] + [swap(own_sum, "group", k) for k in (1, 2, 3)]

    near_head = send(after(pick(bit1, 1 - bit0, 0, cut), own_sum), pair)
    keep = send(after(pick(1 - bit1, 1 - bit0), own_sum), middle)
    near_tail = send(after(pick(bit1, 1 - bit0, cut, tail), own_sum), pair)
    head_rise = send(after(far[:, :cut], own_sum), rise)

    quad = member & 3
    stacked = jnp.stack(turned)
    diag_slices = jnp.stack(
        [lax.dynamic_index_in_dim(stacked, quad ^ g, 0, keepdims=False) for g in range(4)]
    )
    diag = assemble(ids, gather_space(diag_slices))

    half = cross_gram(ids, blocks, far, 0, 3, None, 0)[0]
    half = cross_gram(ids, blocks, near_head, 0, 2, after(half, diag), 0)[0]
    cross_slices = cross_gram(ids, blocks, near_tail, cut, 2, half, parts)
    cross_sum = scatter_space(cross_slices)
    one, two, three = [swap(cross_sum, "group", k) for k in (1, 2, 3)]
    mine = cross_sum + one
    theirs = two + three
    both = jnp.stack([jnp.where(bit1 == 0, mine, theirs), jnp.where(bit1 == 0, theirs, mine)])

    head_leave = send(after(pick(1 - bit1, bit0, 0, cut), both), leave)
    head_pass = send(after(pass_on[:, :cut], both), forward)
    tail_rise = send(after(far[:, cut:], both), rise)
    tail_leave = send(after(pick(1 - bit1, bit0, cut, tail), both), leave)
    tail_pass = send(after(pass_on[:, cut:], both), forward)

    mix, diag = pair_filter(ids, diag, gather_space(both), sketch[0])

    own_head = merge_own(ids, blocks, near_head, 0, mix)
    own_tail = merge_own(ids, blocks, near_tail, cut, mix)
    other_head, half = merge_other(
        ids, [head_leave, keep, head_rise, head_pass], [0] * 4, cut, 0, own_head, mix, None, 0
    )
    results = merge_other(
        ids, [tail_leave, keep, tail_rise, tail_pass], [0, cut, 0, 0], tail, 0, own_tail, mix,
        half, parts,
    )
    other_tail, slices = results[0], results[1:]
    total = scatter_space(slices)
    one, two, three = [swap(total, "group", k) for k in (1, 2, 3)]
    total = (total + one) + (two + three)
    own_merged = jnp.concatenate([own_head, own_tail], axis=1)
    merged, diag_own = merge_filter(
        ids, diag, gather_space(total[None]), sketch[1], 2, own_merged, [other_head, other_tail]
    )

    for level in range(2, levels):
        bit = member >> level & 1
        pairs = merged.reshape(-1, 2, block_rows, width)
        kept = lax.dynamic_index_in_dim(pairs, bit, 1, keepdims=False)
        given = lax.dynamic_index_in_dim(pairs, 1 - bit, 1, keepdims=False)
        got = swap(given, "group", 1 << level)
        diag_got = swap(diag_own, "group", 1 << level)
        lower = jnp.where(bit == 0, kept, got).reshape(-1, width)
        upper = jnp.where(bit == 0, got, kept).reshape(-1, width)
        cross = dot_t(lower, upper).reshape(parts, width // parts, width)
        place = lax.axis_index("space")
        total = scatter_space(
            [lax.dynamic_index_in_dim(cross, place ^ k, 0, keepdims=False) for k in range(parts)],
        )
        for low in range(level + 1):
            total = total + swap(total, "group", 1 << low)
        diag = jnp.stack(
            [jnp.where(bit == 0, diag_own, diag_got), jnp.where(bit == 0, diag_got, diag_own)]
        )
        flag = jnp.stack([lax.axis_index("space"), bit]).astype(jnp.int32)
        merged, diag_own = merge_filter(
            flag, diag, gather_space(total[None]), sketch[level], 1, kept, [got]
        )
    return merged.reshape(block_rows, width)


def solution(mesh):
    in_specs = (P("space", "group"), P())
    out_specs = P(("space", "group"), None)
    return jax.shard_map(compute, mesh=mesh, in_specs=in_specs, out_specs=out_specs, check_vma=False)
```

```python
import functools

import jax
import jax.numpy as jnp
from jax import lax
from jax.experimental import pallas as pl
from jax.experimental.pallas import tpu as pltpu
from jax.sharding import PartitionSpec as P


STEPS = 5
F32 = jnp.float32
BF16 = jnp.bfloat16
HBM = pl.BlockSpec(memory_space=pltpu.HBM)
SMEM = pl.BlockSpec(memory_space=pltpu.SMEM)
VMEM = pl.BlockSpec(memory_space=pltpu.VMEM)


def swap(block, axis, offset):
    count = lax.axis_size(axis)
    return lax.ppermute(block, axis, [(i, i ^ offset) for i in range(count)])


def send(value, routes):
    return lax.ppermute(value, "group", routes)


def after(value, *others):
    return lax.optimization_barrier((value,) + others)[0]


def dot_t(a, b):
    return lax.dot_general(a, b, (((0,), (0,)), ((), ())), preferred_element_type=F32)


def dot(a, b):
    return jnp.dot(a, b, preferred_element_type=F32)


def split(x):
    high = x.astype(BF16)
    return high, (x - high.astype(F32)).astype(BF16)


def dot3(a, b):
    ah, al = a
    bh, bl = b
    return dot(ah, bh) + (dot(ah, bl) + dot(al, bh))


def shape(dims, kind):
    return jax.ShapeDtypeStruct(dims, kind)


def call(kernel, mib, in_specs, outs, scratch, *args):
    return pl.pallas_call(
        kernel,
        in_specs=in_specs,
        out_specs=[VMEM] * len(outs),
        out_shape=outs,
        scratch_shapes=scratch,
        compiler_params=pltpu.CompilerParams(vmem_limit_bytes=mib * 2**20),
    )(*args)


def pick_kernel(cuts, x_ref, *refs):
    outs, sems = refs[:-1], refs[-1]
    groups = lax.axis_size("group")
    block_rows = x_ref.shape[0] // groups
    member = lax.axis_index("group")
    bit0 = member & 1
    bit1 = member >> 1 & 1
    copies = []
    for out, (flip1, flip0, begin) in zip(outs, cuts):
        for h in range(out.shape[0]):
            block = h * 4 + jnp.bitwise_xor(bit1, flip1) * 2 + jnp.bitwise_xor(bit0, flip0)
            start = pl.multiple_of(block * block_rows + begin, 256)
            copies.append(
                pltpu.make_async_copy(
                    x_ref.at[pl.ds(start, out.shape[1]), :], out.at[h], sems.at[len(copies)]
                )
            )
    for copy in copies:
        copy.start()
    for copy in copies:
        copy.wait()


def pick(panel, mib, cuts):
    _, width = panel.shape
    outer = lax.axis_size("group") // 4
    outs = [shape((outer, size, width), BF16) for _, _, _, size in cuts]
    sems = pltpu.SemaphoreType.DMA((len(cuts) * outer,))
    return call(
        functools.partial(pick_kernel, [cut[:3] for cut in cuts]),
        mib, [HBM], outs, [sems], panel,
    )


def place(me, offset, rows, width):
    device = jnp.bitwise_xor(me, offset)
    start = (device & 1) * (width // 2) + (device >> 1) * rows
    return pl.multiple_of(start, rows)


def write_halves(me, acc, mine, sent):
    rows = mine.shape[0]
    mine[...] = acc[pl.ds(pl.multiple_of((me & 1) * rows, rows), rows), :]
    sent[...] = acc[pl.ds(pl.multiple_of((1 - (me & 1)) * rows, rows), rows), :]


def halves(width):
    return [shape((width // 2, width), F32)] * 2


def divide_kernel(x, head, tail):
    head[...] = x[:, : head.shape[1], :]
    tail[...] = x[:, head.shape[1] :, :]


def divide(x, part):
    outer, rows, width = x.shape
    outs = [shape((outer, size, width), x.dtype) for size in (part, rows - part)]
    return call(divide_kernel, 4, [VMEM], outs, [], x)


def own_gram_kernel(ids, *refs):
    blocks, (mine, sent, acc) = refs[:-3], refs[-3:]
    total = None
    for block in blocks:
        for h in range(block.shape[0]):
            x = block[h]
            part = dot_t(x, x)
            total = part if total is None else total + part
    acc[...] = total
    write_halves(ids[0], acc, mine, sent)


def own_gram(ids, blocks):
    width = blocks[0].shape[-1]
    scratch = [pltpu.VMEM((width, width), F32)]
    return call(
        own_gram_kernel, 12, [SMEM] + [VMEM] * len(blocks), halves(width), scratch,
        ids, *blocks,
    )


def cross_kernel(begin, chained, last, ids, own, other, *refs):
    if chained:
        start, refs = refs[0], refs[1:]
    outs, acc = refs[:-1], refs[-1]
    rows = other.shape[1]

    def add(flip):
        total = start[...] if chained else None
        for h in range(other.shape[0]):
            pair = (own[h, begin : begin + rows, :], other[h])
            part = dot_t(pair[flip], pair[1 - flip])
            total = part if total is None else total + part
        acc[...] = total

    pl.when(ids[1] == 0)(lambda: add(0))
    pl.when(ids[1] == 1)(lambda: add(1))
    if last:
        write_halves(ids[0], acc, *outs)
    else:
        outs[0][...] = acc[...]


def cross_gram(ids, own, other, begin, start, last):
    width = own.shape[-1]
    chained = start is not None
    outs = halves(width) if last else [shape((width, width), F32)]
    return call(
        functools.partial(cross_kernel, begin, chained, last),
        8, [SMEM] + [VMEM] * (2 + chained), outs,
        [pltpu.VMEM((width, width), F32)],
        ids, own, other, *([start] if chained else []),
    )


def share_kernel(ids, mine, got, *refs):
    outs, acc = refs[:-1], refs[-1]
    acc[...] = mine[...] + got[...]
    rows = outs[0].shape[0]
    for k, out in enumerate(outs):
        start = pl.multiple_of(jnp.bitwise_xor(ids[0] >> 1, k) * rows, rows)
        out[...] = acc[pl.ds(start, rows), :]


def scatter_space(ids, mine, sent):
    chips = lax.axis_size("space") // 2
    rows, width = mine.shape
    got = swap(sent, "space", 1)
    slices = call(
        share_kernel, 4, [SMEM, VMEM, VMEM],
        [shape((rows // chips, width), F32)] * chips, [pltpu.VMEM((rows, width), F32)],
        ids, mine, got,
    )
    total = slices[0]
    got = [swap(slices[k], "space", 2 * k) for k in range(1, chips)]
    for piece in got:
        total = total + piece
    return total


def gather_space(piece):
    count = lax.axis_size("space")
    pieces = [piece] + [None] * (count - 1)
    for k in range(2, count, 2):
        pieces[k] = swap(piece, "space", k)
    for k in range(0, count, 2):
        pieces[k + 1] = swap(pieces[k], "space", 1)
    return pieces


def assemble_kernel(ids, *refs):
    pieces, out = refs[:-1], refs[-1]
    rows, width = pieces[0].shape[1:]
    for k, piece in enumerate(pieces):
        out[:, pl.ds(place(ids[0], k, rows, width), rows), :] = piece[...]


def assemble(ids, pieces):
    lead, rows, width = pieces[0].shape
    return call(
        assemble_kernel, 4, [SMEM] + [VMEM] * len(pieces),
        [shape((lead, rows * len(pieces), width), F32)], [], ids, *pieces,
    )[0]


def run_filter(pairs, ids, diag, given, pieces, gram, iterate):
    rows, width = pieces[0].shape[1:]
    full = 2 * width
    for p in range(pairs):
        gram[p, :width, :width] = diag[2 * p]
        gram[p, width:, width:] = diag[2 * p + 1]
        for k, piece in enumerate(pieces):
            gram[p, pl.ds(place(ids[0], k, rows, width), rows), width:] = piece[p]
        gram[p, width:, :width] = gram[p, :width, width:].T
    eye = lax.broadcasted_iota(jnp.int32, (full, full), 0) == lax.broadcasted_iota(
        jnp.int32, (full, full), 1
    )
    for p in range(pairs):
        whole = gram[p]
        trace = jnp.sum(jnp.where(eye, whole, 0.0), keepdims=True)
        shifted = whole / (trace / full) - jnp.where(eye, 1.0, 0.0)
        norm = jnp.sqrt(jnp.sum(shifted * shifted, keepdims=True))
        iterate[p] = shifted / (1.0 + norm)

    def step(_, carry):
        xs = [iterate[p] for p in range(pairs)]
        short = [x.astype(BF16) for x in xs]
        squares = [dot(x, x).astype(BF16) for x in short]
        for p in range(pairs):
            iterate[p] = 1.5 * xs[p] - 0.5 * dot(short[p], squares[p])
        return carry

    lax.fori_loop(0, STEPS - 1, step, 0)
    given_parts = split(given)
    parts = [split(iterate[p]) for p in range(pairs)]
    first = [dot3(part, given_parts) for part in parts]
    second = [dot3(part, split(t)) for part, t in zip(parts, first)]
    third = [dot3(part, split(t)) for part, t in zip(parts, second)]
    mixes = []
    for p in range(pairs):
        applied = 1.5 * first[p] - 0.5 * third[p]
        mixes.append((0.5 * (given + applied)).astype(BF16))
    return mixes


def pair_filter_kernel(ids, diag, sketch, *refs):
    pieces, (mix_ref, gram, iterate) = refs[:-3], refs[-3:]
    mixes = run_filter(2, ids, diag, sketch[0], pieces, gram, iterate)
    for p in range(2):
        mix_ref[p] = mixes[p].reshape(mix_ref.shape[1:])


def pair_filter(ids, diag, pieces, sketch):
    pairs, _, width = pieces[0].shape
    outs = [shape((pairs, 2, width, width), BF16), shape((pairs, 2 * width, 2 * width), F32)]
    return call(
        pair_filter_kernel, 20, [SMEM] + [VMEM] * (2 + len(pieces)), outs,
        [pltpu.VMEM((pairs, 2 * width, 2 * width), F32)],
        ids, diag, sketch, *pieces,
    )


def next_diag_kernel(gram, mix, out):
    for p in range(out.shape[0]):
        gh, gl = split(gram[p])
        m = mix[p].reshape(gh.shape[0], -1)
        th, tl = split(dot(gh, m) + dot(gl, m))
        out[p] = dot_t(m, th) + dot_t(m, tl)


def next_diag(gram, mix):
    pairs, _, width, _ = mix.shape
    return call(
        next_diag_kernel, 12, [VMEM] * 2, [shape((pairs, width, width), F32)], [],
        gram, mix,
    )[0]


def read(pieces, h, begin, size):
    for piece in pieces:
        if begin < piece.shape[1]:
            return piece[h, begin : begin + size, :]
        begin -= piece.shape[1]


def merge_own_kernel(ids, mix, mine, near_head, near_tail, out):
    bit0, bit1 = ids[1], ids[2]
    tile = min(512, near_head.shape[1], near_tail.shape[1])
    for h in range(mine.shape[0]):
        for b in range(0, mine.shape[1], tile):
            total = dot(mine[h, b : b + tile, :], mix[bit1, bit0])
            total += dot(read([near_head, near_tail], h, b, tile), mix[bit1, 1 - bit0])
            out[h, b : b + tile, :] = total.astype(BF16)


def merge_own(ids, mix, mine, *near):
    return call(
        merge_own_kernel, 8, [SMEM] + [VMEM] * 4, [shape(mine.shape, BF16)], [],
        ids, mix, mine, *near,
    )[0]


def merge_other_kernel(begin, chained, last, ids, mix, own, left, keep, passed, *refs):
    if chained:
        start, refs = refs[0], refs[1:]
    count = 3 if last else 2
    risen, (out, *outs, acc) = refs[: -count - 1], refs[-count - 1 :]
    bit0, bit1 = ids[1], ids[2]
    pair = 1 - bit1
    acc[...] = start[...] if chained else jnp.zeros(acc.shape, F32)
    outer, rows, _ = out.shape
    tile = min(256, rows)
    tile = 128 if rows % 256 else tile
    tiles = [(h, b) for h in range(outer) for b in range(0, rows, tile)]

    def merge(low, low_begin, high, high_begin):
        for h, b in tiles:
            total = dot(read(low, h, low_begin + b, tile), mix[pair, pair])
            total += dot(read(high, h, high_begin + b, tile), mix[pair, 1 - pair])
            out[h, b : b + tile, :] = total.astype(BF16)

    pl.when(bit0 != bit1)(lambda: merge([left], begin, [keep], begin))
    pl.when(bit0 == bit1)(lambda: merge(risen, begin, [passed], 0))

    def add(flip):
        for h in range(outer):
            both = (own[h, begin : begin + rows, :], out[h])
            acc[...] += dot_t(both[flip], both[1 - flip])

    pl.when(bit1 == 0)(lambda: add(0))
    pl.when(bit1 == 1)(lambda: add(1))
    if last:
        write_halves(ids[0], acc, *outs)
    else:
        outs[0][...] = acc[...]


def merge_other(ids, mix, own, begin, left, keep, passed, risen, start):
    width = own.shape[-1]
    chained = start is not None
    outs = halves(width) if chained else [shape((width, width), F32)]
    args = [ids, mix, own, left, keep, passed] + ([start] if chained else []) + risen
    return call(
        functools.partial(merge_other_kernel, begin, chained, chained), 12,
        [SMEM] + [VMEM] * (len(args) - 1), [shape(passed.shape, BF16)] + outs,
        [pltpu.VMEM((width, width), F32)], *args,
    )


def merge_filter_kernel(which, level, last, cuts, ids, diag, sketch, own, *refs):
    others, refs = refs[:cuts], refs[cuts:]
    count = 3 if last else 4
    pieces, refs = refs[:-count], refs[-count:]
    out, mix_ref, gram, iterate = refs[0], refs[-2 if last else 1], None, refs[-1]
    if last:
        gram = refs[-2]
        mix_ref = None
    else:
        gram = refs[2]
    mix = run_filter(1, ids, diag, sketch[level], pieces, gram, iterate)[0]
    width = diag.shape[-1]
    bit = ids[which]

    def finish(low, high):
        for h in range(own.shape[0]):
            for b in range(0, own.shape[1], tile):
                total = dot(read(low, h, b, tile), mix[:width])
                total += dot(read(high, h, b, tile), mix[width:])
                out[h, b : b + tile, :] = total.astype(BF16)

    tile = min(256, *(other.shape[1] & -other.shape[1] for other in others))
    pl.when(bit == 0)(lambda: finish([own], others))
    pl.when(bit == 1)(lambda: finish(others, [own]))
    if not last:
        mix_ref[0] = mix.reshape(mix_ref.shape[1:])


def merge_filter(ids, which, level, last, diag, pieces, sketch, own, others):
    width = diag.shape[-1]
    square = (1, 2 * width, 2 * width)
    outs = [shape(own.shape, BF16)]
    scratch = [pltpu.VMEM(square, F32)] * 2
    if not last:
        outs += [shape((1, 2, width, width), BF16), shape(square, F32)]
        scratch = scratch[:1]
    return call(
        functools.partial(merge_filter_kernel, which, level, last, len(others)),
        20, [SMEM] + [VMEM] * (3 + len(others) + len(pieces)), outs, scratch,
        ids, diag, sketch, own, *others, *pieces,
    )


def compute(snapshot_basis, sketch):
    rows, width = snapshot_basis.shape
    groups = lax.axis_size("group")
    levels = groups.bit_length() - 1
    member = lax.axis_index("group")
    bit0 = member & 1
    bit1 = member >> 1 & 1
    ids = jnp.stack([lax.axis_index("space"), bit0, bit1]).astype(jnp.int32)
    block_rows = rows // groups
    cut = block_rows * 3 // 4
    tail = block_rows - cut
    part = block_rows // 2

    middle, forward, rise, leave = [], [], [], []
    for base in range(0, groups, 4):
        middle += [(base + 1, base + 2), (base + 2, base + 1)]
        forward += [(base + 1, base), (base + 2, base + 3)]
        rise += [(base + 1, base + 3), (base + 2, base)]
        leave += [(base, base + 2), (base + 3, base + 1)]
    pair = [(i, i ^ 1) for i in range(groups)]

    far_own, across = pick(snapshot_basis, 59, [(1, 1, 0, block_rows), (1, 0, 0, block_rows)])
    far = send(far_own, pair)
    pass_on = send(across, middle)
    cuts = [(0, 1, 0, cut), (0, 1, cut, tail), (0, 0, 0, block_rows)]
    near_own, tail_own, mine = pick(after(snapshot_basis, far_own), 59, cuts)

    own_halves = own_gram(ids, [far_own, across, near_own, tail_own, mine])
    own_sum = scatter_space(ids, *own_halves)
    turned = [own_sum] + [swap(own_sum, "group", k) for k in (1, 2, 3)]

    near_head = send(after(near_own, own_sum), pair)
    keep = send(after(far_own, own_sum), middle)
    near_tail = send(after(tail_own, own_sum), pair)
    far_head, far_tail = divide(far, part)
    rise_head = send(after(far_head, own_sum), rise)

    quad = member & 3
    stacked = jnp.stack(turned)
    diag_slices = jnp.stack(
        [lax.dynamic_index_in_dim(stacked, quad ^ g, 0, keepdims=False) for g in range(4)]
    )
    diag = assemble(ids, gather_space(diag_slices))

    cross = cross_gram(ids, across, far, 0, None, False)[0]
    cross = cross_gram(ids, mine, near_head, 0, cross, False)[0]
    cross_halves = cross_gram(ids, mine, near_tail, cut, cross, True)
    cross_sum = scatter_space(ids, *cross_halves)
    here = cross_sum + send(cross_sum, pair)
    there = swap(here, "group", 2)
    both = jnp.stack([jnp.where(bit1 == 0, here, there), jnp.where(bit1 == 0, there, here)])

    pass_parts = divide(pass_on, cut)
    pass_head = send(after(pass_parts[0], here), forward)
    left = send(after(across, here), leave)
    rise_tail = send(after(far_tail, here), rise)
    pass_tail = send(after(pass_parts[1], here), forward)

    mix, gram = pair_filter(ids, diag, gather_space(both), sketch)
    diag = next_diag(gram, mix)
    own_merged = merge_own(ids, mix, mine, near_head, near_tail)
    other_head, cross = merge_other(
        ids, mix, own_merged, 0, left, keep, pass_head, [rise_head, rise_tail], None
    )
    other_tail, *both_halves = merge_other(
        ids, mix, own_merged, cut, left, keep, pass_tail, [rise_head, rise_tail],
        cross,
    )
    total = scatter_space(ids, *both_halves)
    one, two, three = [swap(total, "group", k) for k in (1, 2, 3)]
    total = (total + one) + (two + three)
    result = merge_filter(
        ids, 2, 1, levels == 2, diag, gather_space(total[None]), sketch,
        own_merged, [other_head, other_tail],
    )

    for level in range(2, levels):
        merged = result[0]
        bit = member >> level & 1
        pairs = merged.reshape(-1, 2, block_rows, width)
        kept = lax.dynamic_index_in_dim(pairs, bit, 1, keepdims=False)
        given = lax.dynamic_index_in_dim(pairs, 1 - bit, 1, keepdims=False)
        got = swap(given, "group", 1 << level)
        diag_own = next_diag(result[2], result[1])[0]
        diag_got = swap(diag_own, "group", 1 << level)
        flags = jnp.stack([lax.axis_index("space"), bit]).astype(jnp.int32)
        total = scatter_space(flags, *cross_gram(flags, kept, got, 0, None, True))
        for low in range(level + 1):
            total = total + swap(total, "group", 1 << low)
        diag = jnp.stack(
            [jnp.where(bit == 0, diag_own, diag_got), jnp.where(bit == 0, diag_got, diag_own)]
        )
        result = merge_filter(
            flags, 1, level, level + 1 == levels, diag, gather_space(total[None]),
            sketch, kept, [got],
        )
    return result[0].reshape(block_rows, width)


def solution(mesh):
    in_specs = (P("space", "group"), P())
    out_specs = P(("space", "group"), None)
    return jax.shard_map(compute, mesh=mesh, in_specs=in_specs, out_specs=out_specs, check_vma=False)
```

```python
import functools
import math

import jax
import jax.numpy as jnp
from jax import lax
from jax.experimental import pallas as pl
from jax.experimental.pallas import tpu as pltpu
from jax.sharding import PartitionSpec as P


STEPS = 5
F32 = jnp.float32
BF16 = jnp.bfloat16
HBM = pl.BlockSpec(memory_space=pltpu.HBM)
SMEM = pl.BlockSpec(memory_space=pltpu.SMEM)
VMEM = pl.BlockSpec(memory_space=pltpu.VMEM)


def swap(block, axis, offset):
    count = lax.axis_size(axis)
    return lax.ppermute(block, axis, [(i, i ^ offset) for i in range(count)])


def send(value, routes):
    return lax.ppermute(value, "group", routes)


def after(value, *others):
    return lax.optimization_barrier((value,) + others)[0]


def dot_t(a, b):
    return lax.dot_general(a, b, (((0,), (0,)), ((), ())), preferred_element_type=F32)


def dot(a, b):
    return jnp.dot(a, b, preferred_element_type=F32)


def split(x):
    high = x.astype(BF16)
    return high, (x - high.astype(F32)).astype(BF16)


def dot3(a, b):
    ah, al = a
    bh, bl = b
    return dot(ah, bh) + (dot(ah, bl) + dot(al, bh))


def shape(dims, kind):
    return jax.ShapeDtypeStruct(dims, kind)


def call(kernel, mib, in_specs, outs, scratch, *args):
    return pl.pallas_call(
        kernel,
        in_specs=in_specs,
        out_specs=[VMEM] * len(outs),
        out_shape=outs,
        scratch_shapes=scratch,
        compiler_params=pltpu.CompilerParams(vmem_limit_bytes=mib * 2**20),
    )(*args)


def pick_kernel(cuts, x_ref, *refs):
    outs, sems = refs[:-1], refs[-1]
    groups = lax.axis_size("group")
    block_rows = x_ref.shape[0] // groups
    member = lax.axis_index("group")
    bit0 = member & 1
    bit1 = member >> 1 & 1
    copies = []
    for out, (flip1, flip0, begin) in zip(outs, cuts):
        for h in range(out.shape[0]):
            block = h * 4 + jnp.bitwise_xor(bit1, flip1) * 2 + jnp.bitwise_xor(bit0, flip0)
            start = pl.multiple_of(block * block_rows + begin, 256)
            copies.append(
                pltpu.make_async_copy(
                    x_ref.at[pl.ds(start, out.shape[1]), :], out.at[h], sems.at[len(copies)]
                )
            )
    for copy in copies:
        copy.start()
    for copy in copies:
        copy.wait()


def pick(panel, mib, cuts):
    _, width = panel.shape
    outer = lax.axis_size("group") // 4
    outs = [shape((outer, size, width), BF16) for _, _, _, size in cuts]
    sems = pltpu.SemaphoreType.DMA((len(cuts) * outer,))
    return call(
        functools.partial(pick_kernel, [cut[:3] for cut in cuts]),
        mib, [HBM], outs, [sems], panel,
    )


def place(me, offset, rows, width):
    device = jnp.bitwise_xor(me, offset)
    start = (device & 1) * (width // 2) + (device >> 1) * rows
    return pl.multiple_of(start, rows)


def write_halves(me, acc, mine, sent):
    rows = mine.shape[0]
    mine[...] = acc[pl.ds(pl.multiple_of((me & 1) * rows, rows), rows), :]
    sent[...] = acc[pl.ds(pl.multiple_of((1 - (me & 1)) * rows, rows), rows), :]


def halves(width):
    return [shape((width // 2, width), F32)] * 2


def divide_kernel(x, head, tail):
    head[...] = x[:, : head.shape[1], :]
    tail[...] = x[:, head.shape[1] :, :]


def divide(x, part):
    outer, rows, width = x.shape
    outs = [shape((outer, size, width), x.dtype) for size in (part, rows - part)]
    return call(divide_kernel, 4, [VMEM], outs, [], x)


def own_gram_kernel(ids, *refs):
    blocks, (mine, sent, acc) = refs[:-3], refs[-3:]
    total = None
    for block in blocks:
        for h in range(block.shape[0]):
            x = block[h]
            part = dot_t(x, x)
            total = part if total is None else total + part
    acc[...] = total
    write_halves(ids[0], acc, mine, sent)


def own_gram(ids, blocks):
    width = blocks[0].shape[-1]
    scratch = [pltpu.VMEM((width, width), F32)]
    return call(
        own_gram_kernel, 12, [SMEM] + [VMEM] * len(blocks), halves(width), scratch,
        ids, *blocks,
    )


def cross_kernel(begin, chained, last, ids, own, other, *refs):
    if chained:
        start, refs = refs[0], refs[1:]
    outs, acc = refs[:-1], refs[-1]
    rows = other.shape[1]

    def add(flip):
        total = start[...] if chained else None
        for h in range(other.shape[0]):
            pair = (own[h, begin : begin + rows, :], other[h])
            part = dot_t(pair[flip], pair[1 - flip])
            total = part if total is None else total + part
        acc[...] = total

    pl.when(ids[1] == 0)(lambda: add(0))
    pl.when(ids[1] == 1)(lambda: add(1))
    if last:
        write_halves(ids[0], acc, *outs)
    else:
        outs[0][...] = acc[...]


def cross_gram(ids, own, other, begin, start, last):
    width = own.shape[-1]
    chained = start is not None
    outs = halves(width) if last else [shape((width, width), F32)]
    return call(
        functools.partial(cross_kernel, begin, chained, last),
        8, [SMEM] + [VMEM] * (2 + chained), outs,
        [pltpu.VMEM((width, width), F32)],
        ids, own, other, *([start] if chained else []),
    )


def share_kernel(ids, mine, got, *refs):
    outs, acc = refs[:-1], refs[-1]
    acc[...] = mine[...] + got[...]
    rows = outs[0].shape[0]
    for k, out in enumerate(outs):
        start = pl.multiple_of(jnp.bitwise_xor(ids[0] >> 1, k) * rows, rows)
        out[...] = acc[pl.ds(start, rows), :]


def scatter_space(ids, mine, sent):
    chips = lax.axis_size("space") // 2
    rows, width = mine.shape
    got = swap(sent, "space", 1)
    slices = call(
        share_kernel, 4, [SMEM, VMEM, VMEM],
        [shape((rows // chips, width), F32)] * chips, [pltpu.VMEM((rows, width), F32)],
        ids, mine, got,
    )
    total = slices[0]
    got = [swap(slices[k], "space", 2 * k) for k in range(1, chips)]
    for piece in got:
        total = total + piece
    return total


def gather_space(piece):
    count = lax.axis_size("space")
    pieces = [piece] + [None] * (count - 1)
    for k in range(2, count, 2):
        pieces[k] = swap(piece, "space", k)
    for k in range(0, count, 2):
        pieces[k + 1] = swap(pieces[k], "space", 1)
    return pieces


def assemble_kernel(ids, *refs):
    pieces, out = refs[:-1], refs[-1]
    rows, width = pieces[0].shape[1:]
    for k, piece in enumerate(pieces):
        out[:, pl.ds(place(ids[0], k, rows, width), rows), :] = piece[...]


def assemble(ids, pieces):
    lead, rows, width = pieces[0].shape
    return call(
        assemble_kernel, 4, [SMEM] + [VMEM] * len(pieces),
        [shape((lead, rows * len(pieces), width), F32)], [], ids, *pieces,
    )[0]


def run_filter(pairs, ids, diag, given, pieces, gram, iterate):
    rows, width = pieces[0].shape[1:]
    full = 2 * width
    for p in range(pairs):
        gram[p, :width, :width] = diag[2 * p]
        gram[p, width:, width:] = diag[2 * p + 1]
        for k, piece in enumerate(pieces):
            gram[p, pl.ds(place(ids[0], k, rows, width), rows), width:] = piece[p]
        gram[p, width:, :width] = gram[p, :width, width:].T
    eye = lax.broadcasted_iota(jnp.int32, (full, full), 0) == lax.broadcasted_iota(
        jnp.int32, (full, full), 1
    )
    for p in range(pairs):
        whole = gram[p]
        trace = jnp.sum(jnp.where(eye, whole, 0.0), keepdims=True)
        shifted = whole / (trace / full) - jnp.where(eye, 1.0, 0.0)
        norm = jnp.sqrt(jnp.sum(shifted * shifted, keepdims=True))
        iterate[p] = shifted / (1.0 + norm)

    def step(_, carry):
        xs = [iterate[p] for p in range(pairs)]
        short = [x.astype(BF16) for x in xs]
        squares = [dot(x, x).astype(BF16) for x in short]
        for p in range(pairs):
            iterate[p] = 1.5 * xs[p] - 0.5 * dot(short[p], squares[p])
        return carry

    lax.fori_loop(0, STEPS - 1, step, 0)
    given_parts = split(given)
    parts = [split(iterate[p]) for p in range(pairs)]
    first = [dot3(part, given_parts) for part in parts]
    second = [dot3(part, split(t)) for part, t in zip(parts, first)]
    third = [dot3(part, split(t)) for part, t in zip(parts, second)]
    mixes = []
    for p in range(pairs):
        applied = 1.5 * first[p] - 0.5 * third[p]
        mixes.append((0.5 * (given + applied)).astype(BF16))
    return mixes


def pair_filter_kernel(ids, diag, sketch, *refs):
    pieces, (mix_ref, gram, iterate) = refs[:-3], refs[-3:]
    mixes = run_filter(2, ids, diag, sketch[0], pieces, gram, iterate)
    for p in range(2):
        mix_ref[p] = mixes[p].reshape(mix_ref.shape[1:])


def pair_filter(ids, diag, pieces, sketch):
    pairs, _, width = pieces[0].shape
    outs = [shape((pairs, 2, width, width), BF16), shape((pairs, 2 * width, 2 * width), F32)]
    return call(
        pair_filter_kernel, 20, [SMEM] + [VMEM] * (2 + len(pieces)), outs,
        [pltpu.VMEM((pairs, 2 * width, 2 * width), F32)],
        ids, diag, sketch, *pieces,
    )


def next_diag_kernel(gram, mix, out):
    for p in range(out.shape[0]):
        gh, gl = split(gram[p])
        m = mix[p].reshape(gh.shape[0], -1)
        th, tl = split(dot(gh, m) + dot(gl, m))
        out[p] = dot_t(m, th) + dot_t(m, tl)


def next_diag(gram, mix):
    pairs, _, width, _ = mix.shape
    return call(
        next_diag_kernel, 12, [VMEM] * 2, [shape((pairs, width, width), F32)], [],
        gram, mix,
    )[0]


def read(pieces, h, begin, size):
    for piece in pieces:
        if begin < piece.shape[1]:
            return piece[h, begin : begin + size, :]
        begin -= piece.shape[1]


def merge_own_kernel(ids, mix, mine, near_head, near_tail, out):
    bit0, bit1 = ids[1], ids[2]
    tile = math.gcd(512, near_head.shape[1], near_tail.shape[1])
    for h in range(mine.shape[0]):
        for b in range(0, mine.shape[1], tile):
            total = dot(mine[h, b : b + tile, :], mix[bit1, bit0])
            total += dot(read([near_head, near_tail], h, b, tile), mix[bit1, 1 - bit0])
            out[h, b : b + tile, :] = total.astype(BF16)


def merge_own(ids, mix, mine, *near):
    return call(
        merge_own_kernel, 8, [SMEM] + [VMEM] * 4, [shape(mine.shape, BF16)], [],
        ids, mix, mine, *near,
    )[0]


def merge_other_kernel(begin, segments, chained, ids, mix, own, keep, risen, *refs):
    count = len(segments)
    left, passed, refs = refs[:count], refs[count : 2 * count], refs[2 * count :]
    if chained:
        start, refs = refs[0], refs[1:]
    out, *outs, acc = refs
    bit0, bit1 = ids[1], ids[2]
    pair = 1 - bit1
    acc[...] = start[...] if chained else jnp.zeros(acc.shape, F32)
    outer, total_rows, _ = out.shape

    def merge(outer_of, inner_of):
        at = 0
        for k, (skip, rows) in enumerate(segments):
            for h in range(outer):
                total = dot(outer_of(k, h, skip, rows, at), mix[pair, pair])
                total += dot(inner_of(k, h, skip, rows, at), mix[pair, 1 - pair])
                out[h, at : at + rows, :] = total.astype(BF16)
            at += rows

    def near():
        merge(
            lambda k, h, skip, rows, at: left[k][h, skip : skip + rows, :],
            lambda k, h, skip, rows, at: keep[h, begin + at : begin + at + rows, :],
        )

    def distant():
        merge(
            lambda k, h, skip, rows, at: risen[h, at : at + rows, :],
            lambda k, h, skip, rows, at: passed[k][h, skip : skip + rows, :],
        )

    pl.when(bit0 != bit1)(near)
    pl.when(bit0 == bit1)(distant)

    def add(flip):
        for h in range(outer):
            both = (own[h, begin : begin + total_rows, :], out[h])
            acc[...] += dot_t(both[flip], both[1 - flip])

    pl.when(bit1 == 0)(lambda: add(0))
    pl.when(bit1 == 1)(lambda: add(1))
    if chained:
        write_halves(ids[0], acc, *outs)
    else:
        outs[0][...] = acc[...]


def merge_other(begin, segments, start, ids, mix, own, keep, risen, left, passed):
    outer, _, width = own.shape
    chained = start is not None
    outs = halves(width) if chained else [shape((width, width), F32)]
    args = [ids, mix, own, keep, risen, *left, *passed] + ([start] if chained else [])
    rows = sum(size for _, size in segments)
    return call(
        functools.partial(merge_other_kernel, begin, segments, chained), 12,
        [SMEM] + [VMEM] * (len(args) - 1), [shape((outer, rows, width), BF16)] + outs,
        [pltpu.VMEM((width, width), F32)], *args,
    )


def merge_filter_kernel(which, level, last, cuts, ids, diag, sketch, own, *refs):
    others, refs = refs[:cuts], refs[cuts:]
    count = 3 if last else 4
    pieces, refs = refs[:-count], refs[-count:]
    out, mix_ref, gram, iterate = refs[0], refs[-2 if last else 1], None, refs[-1]
    if last:
        gram = refs[-2]
        mix_ref = None
    else:
        gram = refs[2]
    mix = run_filter(1, ids, diag, sketch[level], pieces, gram, iterate)[0]
    width = diag.shape[-1]
    bit = ids[which]

    def finish(low, high):
        for h in range(own.shape[0]):
            for b in range(0, own.shape[1], tile):
                total = dot(read(low, h, b, tile), mix[:width])
                total += dot(read(high, h, b, tile), mix[width:])
                out[h, b : b + tile, :] = total.astype(BF16)

    tile = math.gcd(256, *(other.shape[1] for other in others))
    pl.when(bit == 0)(lambda: finish([own], others))
    pl.when(bit == 1)(lambda: finish(others, [own]))
    if not last:
        mix_ref[0] = mix.reshape(mix_ref.shape[1:])


def merge_filter(ids, which, level, last, diag, pieces, sketch, own, others):
    width = diag.shape[-1]
    square = (1, 2 * width, 2 * width)
    outs = [shape(own.shape, BF16)]
    scratch = [pltpu.VMEM(square, F32)] * 2
    if not last:
        outs += [shape((1, 2, width, width), BF16), shape(square, F32)]
        scratch = scratch[:1]
    return call(
        functools.partial(merge_filter_kernel, which, level, last, len(others)),
        20, [SMEM] + [VMEM] * (3 + len(others) + len(pieces)), outs, scratch,
        ids, diag, sketch, own, *others, *pieces,
    )


def compute(snapshot_basis, sketch):
    rows, width = snapshot_basis.shape
    groups = lax.axis_size("group")
    levels = groups.bit_length() - 1
    member = lax.axis_index("group")
    bit0 = member & 1
    bit1 = member >> 1 & 1
    ids = jnp.stack([lax.axis_index("space"), bit0, bit1]).astype(jnp.int32)
    block_rows = rows // groups
    cut = block_rows * 3 // 4
    tail = block_rows - cut
    part = block_rows * 7 // 16

    middle, forward, rise, leave = [], [], [], []
    for base in range(0, groups, 4):
        middle += [(base + 1, base + 2), (base + 2, base + 1)]
        forward += [(base + 1, base), (base + 2, base + 3)]
        rise += [(base + 1, base + 3), (base + 2, base)]
        leave += [(base, base + 2), (base + 3, base + 1)]
    pair = [(i, i ^ 1) for i in range(groups)]

    far_own, across = pick(snapshot_basis, 48, [(1, 1, 0, block_rows), (1, 0, 0, block_rows)])
    far = send(far_own, pair)
    pass_on = send(across, middle)
    cuts = [(0, 1, 0, cut), (0, 1, cut, tail), (0, 0, 0, block_rows), (1, 0, 0, cut),
            (1, 0, cut, tail)]
    near_own, tail_own, mine, leave_head, leave_tail = pick(after(snapshot_basis, far_own), 48, cuts)

    own_halves = own_gram(ids, [far_own, across, near_own, tail_own, mine])
    own_sum = scatter_space(ids, *own_halves)
    turned = [own_sum] + [swap(own_sum, "group", k) for k in (1, 2, 3)]

    near_head = send(after(near_own, own_sum), pair)
    keep = send(after(far_own, own_sum), middle)
    near_tail = send(after(tail_own, own_sum), pair)
    far_head, far_tail = divide(far, part)
    rise_head = send(after(far_head, own_sum), rise)

    quad = member & 3
    stacked = jnp.stack(turned)
    diag_slices = jnp.stack(
        [lax.dynamic_index_in_dim(stacked, quad ^ g, 0, keepdims=False) for g in range(4)]
    )
    diag = assemble(ids, gather_space(diag_slices))

    cross = cross_gram(ids, across, far, 0, None, False)[0]
    cross = cross_gram(ids, mine, near_head, 0, cross, False)[0]
    cross_halves = cross_gram(ids, mine, near_tail, cut, cross, True)
    cross_sum = scatter_space(ids, *cross_halves)
    one, two, three = [swap(cross_sum, "group", k) for k in (1, 2, 3)]
    here = cross_sum + one
    there = two + three
    both = jnp.stack([jnp.where(bit1 == 0, here, there), jnp.where(bit1 == 0, there, here)])

    pass_parts = divide(pass_on, cut)
    left_head = send(after(leave_head, cross_sum), leave)
    pass_head = send(after(pass_parts[0], cross_sum), forward)
    rise_tail = send(after(far_tail, cross_sum), rise)
    left_tail = send(after(leave_tail, cross_sum), leave)
    pass_tail = send(after(pass_parts[1], cross_sum), forward)

    mix, gram = pair_filter(ids, diag, gather_space(both), sketch)
    diag = next_diag(gram, mix)
    own_merged = merge_own(ids, mix, mine, near_head, near_tail)
    args = [ids, mix, own_merged, keep]
    other_head, cross = merge_other(
        0, [(0, part)], None, *args, rise_head, [left_head], [pass_head]
    )
    other_tail, *both_halves = merge_other(
        part, [(part, cut - part), (0, tail)], cross, *args, rise_tail,
        [left_head, left_tail], [pass_head, pass_tail],
    )
    total = scatter_space(ids, *both_halves)
    one, two, three = [swap(total, "group", k) for k in (1, 2, 3)]
    total = (total + one) + (two + three)
    result = merge_filter(
        ids, 2, 1, levels == 2, diag, gather_space(total[None]), sketch,
        own_merged, [other_head, other_tail],
    )

    for level in range(2, levels):
        merged = result[0]
        bit = member >> level & 1
        pairs = merged.reshape(-1, 2, block_rows, width)
        kept = lax.dynamic_index_in_dim(pairs, bit, 1, keepdims=False)
        given = lax.dynamic_index_in_dim(pairs, 1 - bit, 1, keepdims=False)
        got = swap(given, "group", 1 << level)
        diag_own = next_diag(result[2], result[1])[0]
        diag_got = swap(diag_own, "group", 1 << level)
        flags = jnp.stack([lax.axis_index("space"), bit]).astype(jnp.int32)
        total = scatter_space(flags, *cross_gram(flags, kept, got, 0, None, True))
        for low in range(level + 1):
            total = total + swap(total, "group", 1 << low)
        diag = jnp.stack(
            [jnp.where(bit == 0, diag_own, diag_got), jnp.where(bit == 0, diag_got, diag_own)]
        )
        result = merge_filter(
            flags, 1, level, level + 1 == levels, diag, gather_space(total[None]),
            sketch, kept, [got],
        )
    return result[0].reshape(block_rows, width)


def solution(mesh):
    in_specs = (P("space", "group"), P())
    out_specs = P(("space", "group"), None)
    return jax.shard_map(compute, mesh=mesh, in_specs=in_specs, out_specs=out_specs, check_vma=False)
```

```python
import functools
import math

import jax
import jax.numpy as jnp
from jax import lax
from jax.experimental import pallas as pl
from jax.experimental.pallas import tpu as pltpu
from jax.sharding import PartitionSpec as P


STEPS = 5
F32 = jnp.float32
BF16 = jnp.bfloat16
HBM = pl.BlockSpec(memory_space=pltpu.HBM)
VMEM = pl.BlockSpec(memory_space=pltpu.VMEM)


def swap(block, axis, offset):
    count = lax.axis_size(axis)
    return lax.ppermute(block, axis, [(i, i ^ offset) for i in range(count)])


def send(value, routes):
    return lax.ppermute(value, "group", routes)


def after(value, *others):
    return lax.optimization_barrier((value,) + others)[0]


def dot_t(a, b):
    return lax.dot_general(a, b, (((0,), (0,)), ((), ())), preferred_element_type=F32)


def dot(a, b):
    return jnp.dot(a, b, preferred_element_type=F32)


def split(x):
    high = x.astype(BF16)
    return high, (x - high.astype(F32)).astype(BF16)


def dot3(a, b):
    ah, al = a
    bh, bl = b
    return dot(ah, bh) + (dot(ah, bl) + dot(al, bh))


def shape(dims, kind):
    return jax.ShapeDtypeStruct(dims, kind)


def call(kernel, mib, in_specs, outs, scratch, *args):
    return pl.pallas_call(
        kernel,
        in_specs=in_specs,
        out_specs=[VMEM] * len(outs),
        out_shape=outs,
        scratch_shapes=scratch,
        compiler_params=pltpu.CompilerParams(vmem_limit_bytes=mib * 2**20),
    )(*args)


def pick_kernel(cuts, x_ref, *refs):
    outs, sems = refs[:-1], refs[-1]
    groups = lax.axis_size("group")
    block_rows = x_ref.shape[0] // groups
    member = lax.axis_index("group")
    bit0 = member & 1
    bit1 = member >> 1 & 1
    copies = []
    for out, (flip1, flip0, begin) in zip(outs, cuts):
        for h in range(out.shape[0]):
            block = h * 4 + jnp.bitwise_xor(bit1, flip1) * 2 + jnp.bitwise_xor(bit0, flip0)
            start = pl.multiple_of(block * block_rows + begin, 256)
            copies.append(
                pltpu.make_async_copy(
                    x_ref.at[pl.ds(start, out.shape[1]), :], out.at[h], sems.at[len(copies)]
                )
            )
    for copy in copies:
        copy.start()
    for copy in copies:
        copy.wait()


def pick(panel, mib, cuts):
    _, width = panel.shape
    outer = lax.axis_size("group") // 4
    outs = [shape((outer, size, width), BF16) for _, _, _, size in cuts]
    sems = pltpu.SemaphoreType.DMA((len(cuts) * outer,))
    return call(
        functools.partial(pick_kernel, [cut[:3] for cut in cuts]),
        mib, [HBM], outs, [sems], panel,
    )


def place(offset, rows, width):
    device = jnp.bitwise_xor(where()[0], offset)
    start = (device & 1) * (width // 2) + (device >> 1) * rows
    return pl.multiple_of(start, rows)


def where():
    member = lax.axis_index("group")
    return lax.axis_index("space"), member & 1, member >> 1 & 1


def write_halves(acc, mine, sent):
    me = where()[0]
    rows = mine.shape[0]
    mine[...] = acc[pl.ds(pl.multiple_of((me & 1) * rows, rows), rows), :]
    sent[...] = acc[pl.ds(pl.multiple_of((1 - (me & 1)) * rows, rows), rows), :]


def halves(width):
    return [shape((width // 2, width), F32)] * 2


def divide_kernel(x, head, tail):
    head[...] = x[:, : head.shape[1], :]
    tail[...] = x[:, head.shape[1] :, :]


def divide(x, part):
    outer, rows, width = x.shape
    outs = [shape((outer, size, width), x.dtype) for size in (part, rows - part)]
    return call(divide_kernel, 4, [VMEM], outs, [], x)


def own_gram_kernel(*refs):
    blocks, (mine, sent, acc) = refs[:-3], refs[-3:]
    total = None
    for block in blocks:
        for h in range(block.shape[0]):
            x = block[h]
            part = dot_t(x, x)
            total = part if total is None else total + part
    acc[...] = total
    write_halves(acc, mine, sent)


def own_gram(blocks):
    width = blocks[0].shape[-1]
    scratch = [pltpu.VMEM((width, width), F32)]
    return call(own_gram_kernel, 12, [VMEM] * len(blocks), halves(width), scratch, *blocks)


def cross_kernel(begin, level, chained, last, own, other, *refs):
    if chained:
        start, refs = refs[0], refs[1:]
    outs, acc = refs[:-1], refs[-1]
    rows = other.shape[1]

    def add(flip):
        total = start[...] if chained else None
        for h in range(other.shape[0]):
            pair = (own[h, begin : begin + rows, :], other[h])
            part = dot_t(pair[flip], pair[1 - flip])
            total = part if total is None else total + part
        acc[...] = total

    bit = lax.axis_index("group") >> level & 1
    pl.when(bit == 0)(lambda: add(0))
    pl.when(bit == 1)(lambda: add(1))
    if last:
        write_halves(acc, *outs)
    else:
        outs[0][...] = acc[...]


def cross_gram(own, other, begin, level, start, last):
    width = own.shape[-1]
    chained = start is not None
    outs = halves(width) if last else [shape((width, width), F32)]
    return call(
        functools.partial(cross_kernel, begin, level, chained, last),
        8, [VMEM] * (2 + chained), outs,
        [pltpu.VMEM((width, width), F32)],
        own, other, *([start] if chained else []),
    )


def share_kernel(mine, got, *refs):
    outs, acc = refs[:-1], refs[-1]
    acc[...] = mine[...] + got[...]
    rows = outs[0].shape[0]
    for k, out in enumerate(outs):
        start = pl.multiple_of(jnp.bitwise_xor(where()[0] >> 1, k) * rows, rows)
        out[...] = acc[pl.ds(start, rows), :]


def scatter_space(mine, sent):
    chips = lax.axis_size("space") // 2
    rows, width = mine.shape
    got = swap(sent, "space", 1)
    slices = call(
        share_kernel, 4, [VMEM, VMEM],
        [shape((rows // chips, width), F32)] * chips, [pltpu.VMEM((rows, width), F32)],
        mine, got,
    )
    total = slices[0]
    got = [swap(slices[k], "space", 2 * k) for k in range(1, chips)]
    for piece in got:
        total = total + piece
    return total


def gather_space(piece):
    count = lax.axis_size("space")
    pieces = [piece] + [None] * (count - 1)
    for k in range(2, count, 2):
        pieces[k] = swap(piece, "space", k)
    for k in range(0, count, 2):
        pieces[k + 1] = swap(pieces[k], "space", 1)
    return pieces


def assemble_kernel(*refs):
    pieces, out = refs[:-1], refs[-1]
    rows, width = pieces[0].shape[1:]
    for k, piece in enumerate(pieces):
        out[:, pl.ds(place(k, rows, width), rows), :] = piece[...]


def assemble(pieces):
    lead, rows, width = pieces[0].shape
    return call(
        assemble_kernel, 4, [VMEM] * len(pieces),
        [shape((lead, rows * len(pieces), width), F32)], [], *pieces,
    )[0]


def run_filter(pairs, diag, given, pieces, gram, iterate):
    rows, width = pieces[0].shape[1:]
    full = 2 * width
    for p in range(pairs):
        gram[p, :width, :width] = diag[2 * p]
        gram[p, width:, width:] = diag[2 * p + 1]
        for k, piece in enumerate(pieces):
            gram[p, pl.ds(place(k, rows, width), rows), width:] = piece[p]
        gram[p, width:, :width] = gram[p, :width, width:].T
    eye = lax.broadcasted_iota(jnp.int32, (full, full), 0) == lax.broadcasted_iota(
        jnp.int32, (full, full), 1
    )
    for p in range(pairs):
        whole = gram[p]
        trace = jnp.sum(jnp.where(eye, whole, 0.0), keepdims=True)
        shifted = whole / (trace / full) - jnp.where(eye, 1.0, 0.0)
        norm = jnp.sqrt(jnp.sum(shifted * shifted, keepdims=True))
        iterate[p] = shifted / (1.0 + norm)

    def step(_, carry):
        xs = [iterate[p] for p in range(pairs)]
        short = [x.astype(BF16) for x in xs]
        squares = [dot(x, x).astype(BF16) for x in short]
        for p in range(pairs):
            iterate[p] = 1.5 * xs[p] - 0.5 * dot(short[p], squares[p])
        return carry

    lax.fori_loop(0, STEPS - 1, step, 0)
    given_parts = split(given)
    parts = [split(iterate[p]) for p in range(pairs)]
    first = [dot3(part, given_parts) for part in parts]
    second = [dot3(part, split(t)) for part, t in zip(parts, first)]
    third = [dot3(part, split(t)) for part, t in zip(parts, second)]
    mixes = []
    for p in range(pairs):
        applied = 1.5 * first[p] - 0.5 * third[p]
        mixes.append((0.5 * (given + applied)).astype(BF16))
    return mixes


def pair_filter_kernel(diag, sketch, *refs):
    pieces, (mix_ref, gram, iterate) = refs[:-3], refs[-3:]
    mixes = run_filter(2, diag, sketch[0], pieces, gram, iterate)
    for p in range(2):
        mix_ref[p] = mixes[p].reshape(mix_ref.shape[1:])


def pair_filter(diag, pieces, sketch):
    pairs, _, width = pieces[0].shape
    outs = [shape((pairs, 2, width, width), BF16), shape((pairs, 2 * width, 2 * width), F32)]
    return call(
        pair_filter_kernel, 20, [VMEM] * (2 + len(pieces)), outs,
        [pltpu.VMEM((pairs, 2 * width, 2 * width), F32)],
        diag, sketch, *pieces,
    )


def next_diag_kernel(gram, mix, out):
    for p in range(out.shape[0]):
        gh, gl = split(gram[p])
        m = mix[p].reshape(gh.shape[0], -1)
        th, tl = split(dot(gh, m) + dot(gl, m))
        out[p] = dot_t(m, th) + dot_t(m, tl)


def next_diag(gram, mix):
    pairs, _, width, _ = mix.shape
    return call(
        next_diag_kernel, 12, [VMEM] * 2, [shape((pairs, width, width), F32)], [],
        gram, mix,
    )[0]


def read(pieces, h, begin, size):
    for piece in pieces:
        if begin < piece.shape[1]:
            return piece[h, begin : begin + size, :]
        begin -= piece.shape[1]


def merge_own_kernel(mix, mine, near_head, near_tail, out):
    _, bit0, bit1 = where()
    tile = math.gcd(512, near_head.shape[1], near_tail.shape[1])
    for h in range(mine.shape[0]):
        for b in range(0, mine.shape[1], tile):
            total = dot(mine[h, b : b + tile, :], mix[bit1, bit0])
            total += dot(read([near_head, near_tail], h, b, tile), mix[bit1, 1 - bit0])
            out[h, b : b + tile, :] = total.astype(BF16)


def merge_own(mix, mine, *near):
    return call(
        merge_own_kernel, 8, [VMEM] * 4, [shape(mine.shape, BF16)], [],
        mix, mine, *near,
    )[0]


def merge_other_kernel(begin, segments, chained, mix, own, keep, risen, *refs):
    count = len(segments)
    left, passed, refs = refs[:count], refs[count : 2 * count], refs[2 * count :]
    if chained:
        start, refs = refs[0], refs[1:]
    out, *outs, acc = refs
    _, bit0, bit1 = where()
    pair = 1 - bit1
    acc[...] = start[...] if chained else jnp.zeros(acc.shape, F32)
    outer, total_rows, _ = out.shape

    def merge(outer_of, inner_of):
        at = 0
        for k, (skip, rows) in enumerate(segments):
            for h in range(outer):
                total = dot(outer_of(k, h, skip, rows, at), mix[pair, pair])
                total += dot(inner_of(k, h, skip, rows, at), mix[pair, 1 - pair])
                out[h, at : at + rows, :] = total.astype(BF16)
            at += rows

    def near():
        merge(
            lambda k, h, skip, rows, at: left[k][h, skip : skip + rows, :],
            lambda k, h, skip, rows, at: keep[h, at : at + rows, :],
        )

    def distant():
        merge(
            lambda k, h, skip, rows, at: risen[h, at : at + rows, :],
            lambda k, h, skip, rows, at: passed[k][h, skip : skip + rows, :],
        )

    pl.when(bit0 != bit1)(near)
    pl.when(bit0 == bit1)(distant)

    def add(flip):
        for h in range(outer):
            both = (own[h, begin : begin + total_rows, :], out[h])
            acc[...] += dot_t(both[flip], both[1 - flip])

    pl.when(bit1 == 0)(lambda: add(0))
    pl.when(bit1 == 1)(lambda: add(1))
    if chained:
        write_halves(acc, *outs)
    else:
        outs[0][...] = acc[...]


def merge_other(begin, segments, start, mix, own, keep, risen, left, passed):
    outer, _, width = own.shape
    chained = start is not None
    outs = halves(width) if chained else [shape((width, width), F32)]
    args = [mix, own, keep, risen, *left, *passed] + ([start] if chained else [])
    rows = sum(size for _, size in segments)
    return call(
        functools.partial(merge_other_kernel, begin, segments, chained), 12,
        [VMEM] * len(args), [shape((outer, rows, width), BF16)] + outs,
        [pltpu.VMEM((width, width), F32)], *args,
    )


def merge_filter_kernel(level, last, cuts, diag, sketch, own, *refs):
    others, refs = refs[:cuts], refs[cuts:]
    count = 5 if last else 6
    pieces, (out, *refs, stage, sems) = refs[:-count], refs[-count:]
    gram, iterate = refs[-2:]
    mix = run_filter(1, diag, sketch[level], pieces, gram, iterate)[0]
    width = diag.shape[-1]
    bit = lax.axis_index("group") >> level & 1
    tiles = []
    for other in others:
        begin = tiles[-1][2] + tiles[-1][3] if tiles else 0
        size = math.gcd(512, other.shape[1]) if other.shape[1] <= 512 else other.shape[1] // 2
        for skip in range(0, other.shape[1], size):
            tiles.append((other, skip, begin + skip, size))
    copies = []
    for _, _, begin, size in tiles:
        for h in range(own.shape[0]):
            here = pl.ds(begin, size)
            copies.append(
                pltpu.make_async_copy(
                    stage.at[h, here, :], out.at[h, here, :], sems.at[len(copies)]
                )
            )

    def finish(own_mix, other_mix):
        for k, (other, skip, begin, size) in enumerate(tiles):
            for h in range(own.shape[0]):
                total = dot(own[h, begin : begin + size, :], own_mix)
                total += dot(other[h, skip : skip + size, :], other_mix)
                stage[h, begin : begin + size, :] = total.astype(BF16)
                copies[k * own.shape[0] + h].start()

    pl.when(bit == 0)(lambda: finish(mix[:width], mix[width:]))
    pl.when(bit == 1)(lambda: finish(mix[width:], mix[:width]))
    if not last:
        refs[0][0] = mix.reshape(refs[0].shape[1:])
    for copy in copies:
        copy.wait()


def merge_filter(level, last, diag, pieces, sketch, own, others):
    width = diag.shape[-1]
    square = (1, 2 * width, 2 * width)
    outs = [shape(own.shape, BF16)]
    scratch = [pltpu.VMEM(square, F32)] * 2
    if not last:
        outs += [shape((1, 2, width, width), BF16), shape(square, F32)]
        scratch = scratch[:1]
    count = own.shape[0] * 4 * len(others)
    scratch += [pltpu.VMEM(own.shape, BF16), pltpu.SemaphoreType.DMA((count,))]
    return pl.pallas_call(
        functools.partial(merge_filter_kernel, level, last, len(others)),
        in_specs=[VMEM] * (3 + len(others) + len(pieces)),
        out_specs=[HBM] + [VMEM] * (len(outs) - 1),
        out_shape=outs,
        scratch_shapes=scratch,
        compiler_params=pltpu.CompilerParams(vmem_limit_bytes=20 * 2**20),
        name="merge_filter",
    )(diag, sketch, own, *others, *pieces)


def compute(snapshot_basis, sketch):
    rows, width = snapshot_basis.shape
    groups = lax.axis_size("group")
    levels = groups.bit_length() - 1
    member = lax.axis_index("group")
    bit1 = member >> 1 & 1
    block_rows = rows // groups
    cut = block_rows * 3 // 4
    tail = block_rows - cut
    part = block_rows * 3 // 8

    middle, forward, rise, leave = [], [], [], []
    for base in range(0, groups, 4):
        middle += [(base + 1, base + 2), (base + 2, base + 1)]
        forward += [(base + 1, base), (base + 2, base + 3)]
        rise += [(base + 1, base + 3), (base + 2, base)]
        leave += [(base, base + 2), (base + 3, base + 1)]
    pair = [(i, i ^ 1) for i in range(groups)]

    far_own, across = pick(snapshot_basis, 48, [(1, 1, 0, block_rows), (1, 0, 0, block_rows)])
    far = send(far_own, pair)
    pass_on = send(across, middle)
    cuts = [(0, 1, 0, cut), (0, 1, cut, tail), (0, 0, 0, block_rows), (1, 0, 0, cut),
            (1, 0, cut, tail)]
    near_own, tail_own, mine, leave_head, leave_tail = pick(after(snapshot_basis, far_own), 48, cuts)

    own_halves = own_gram([far_own, across, near_own, tail_own, mine])
    own_sum = scatter_space(*own_halves)
    turned = [own_sum] + [swap(own_sum, "group", k) for k in (1, 2, 3)]

    near_head = send(after(near_own, own_sum), pair)
    keep = send(after(far_own, own_sum), middle)
    near_tail = send(after(tail_own, own_sum), pair)
    far_head, far_tail = divide(far, part)
    rise_head = send(after(far_head, own_sum), rise)

    quad = member & 3
    stacked = jnp.stack(turned)
    diag_slices = jnp.stack(
        [lax.dynamic_index_in_dim(stacked, quad ^ g, 0, keepdims=False) for g in range(4)]
    )
    diag = assemble(gather_space(diag_slices))

    cross = cross_gram(across, far, 0, 0, None, False)[0]
    cross = cross_gram(mine, near_head, 0, 0, cross, False)[0]
    cross_halves = cross_gram(mine, near_tail, cut, 0, cross, True)
    cross_sum = scatter_space(*cross_halves)
    one, two, three = [swap(cross_sum, "group", k) for k in (1, 2, 3)]
    here = cross_sum + one
    there = two + three
    both = jnp.stack([jnp.where(bit1 == 0, here, there), jnp.where(bit1 == 0, there, here)])

    pass_parts = divide(pass_on, cut)
    left_head = send(after(leave_head, cross_sum), leave)
    pass_head = send(after(pass_parts[0], cross_sum), forward)
    rise_tail = send(after(far_tail, cross_sum), rise)
    left_tail = send(after(leave_tail, cross_sum), leave)
    pass_tail = send(after(pass_parts[1], cross_sum), forward)

    mix, gram = pair_filter(diag, gather_space(both), sketch)
    diag = next_diag(gram, mix)
    own_merged = merge_own(mix, mine, near_head, near_tail)
    args = [mix, own_merged]
    keep_head, keep_tail = divide(keep, part)
    other_head, cross = merge_other(
        0, [(0, part)], None, *args, keep_head, rise_head, [left_head], [pass_head]
    )
    other_tail, *both_halves = merge_other(
        part, [(part, cut - part), (0, tail)], cross, *args, keep_tail, rise_tail,
        [left_head, left_tail], [pass_head, pass_tail],
    )
    total = scatter_space(*both_halves)
    one, two, three = [swap(total, "group", k) for k in (1, 2, 3)]
    total = (total + one) + (two + three)
    result = merge_filter(
        1, levels == 2, diag, gather_space(total[None]), sketch,
        own_merged, [other_head, other_tail],
    )

    for level in range(2, levels):
        merged = result[0]
        bit = member >> level & 1
        pairs = merged.reshape(-1, 2, block_rows, width)
        kept = lax.dynamic_index_in_dim(pairs, bit, 1, keepdims=False)
        given = lax.dynamic_index_in_dim(pairs, 1 - bit, 1, keepdims=False)
        got = swap(given, "group", 1 << level)
        diag_own = next_diag(result[2], result[1])[0]
        diag_got = swap(diag_own, "group", 1 << level)
        total = scatter_space(*cross_gram(kept, got, 0, level, None, True))
        for low in range(level + 1):
            total = total + swap(total, "group", 1 << low)
        diag = jnp.stack(
            [jnp.where(bit == 0, diag_own, diag_got), jnp.where(bit == 0, diag_got, diag_own)]
        )
        result = merge_filter(
            level, level + 1 == levels, diag, gather_space(total[None]),
            sketch, kept, [got],
        )
    return result[0].reshape(block_rows, width)


def solution(mesh):
    in_specs = (P("space", "group"), P())
    out_specs = P(("space", "group"), None)
    return jax.shard_map(compute, mesh=mesh, in_specs=in_specs, out_specs=out_specs, check_vma=False)
```

```python
import functools
import math

import jax
import jax.numpy as jnp
from jax import lax
from jax.experimental import pallas as pl
from jax.experimental.pallas import tpu as pltpu
from jax.sharding import PartitionSpec as P


STEPS = 5
F32 = jnp.float32
BF16 = jnp.bfloat16
HBM = pl.BlockSpec(memory_space=pltpu.HBM)
VMEM = pl.BlockSpec(memory_space=pltpu.VMEM)


def swap(block, axis, offset):
    count = lax.axis_size(axis)
    return lax.ppermute(block, axis, [(i, i ^ offset) for i in range(count)])


def send(value, routes):
    return lax.ppermute(value, "group", routes)


def after(value, *others):
    return lax.optimization_barrier((value,) + others)[0]


def dot_t(a, b):
    return lax.dot_general(a, b, (((0,), (0,)), ((), ())), preferred_element_type=F32)


def dot(a, b):
    return jnp.dot(a, b, preferred_element_type=F32)


def split(x):
    high = x.astype(BF16)
    return high, (x - high.astype(F32)).astype(BF16)


def dot3(a, b):
    ah, al = a
    bh, bl = b
    return dot(ah, bh) + (dot(ah, bl) + dot(al, bh))


def shape(dims, kind):
    return jax.ShapeDtypeStruct(dims, kind)


def call(kernel, mib, in_specs, outs, scratch, *args):
    return pl.pallas_call(
        kernel,
        in_specs=in_specs,
        out_specs=[VMEM] * len(outs),
        out_shape=outs,
        scratch_shapes=scratch,
        compiler_params=pltpu.CompilerParams(vmem_limit_bytes=mib * 2**20),
    )(*args)


def pick_kernel(cuts, x_ref, *refs):
    outs, sems = refs[:-1], refs[-1]
    groups = lax.axis_size("group")
    block_rows = x_ref.shape[0] // groups
    member = lax.axis_index("group")
    bit0 = member & 1
    bit1 = member >> 1 & 1
    copies = []
    for out, (flip1, flip0, begin) in zip(outs, cuts):
        for h in range(out.shape[0]):
            block = h * 4 + jnp.bitwise_xor(bit1, flip1) * 2 + jnp.bitwise_xor(bit0, flip0)
            start = pl.multiple_of(block * block_rows + begin, 256)
            copies.append(
                pltpu.make_async_copy(
                    x_ref.at[pl.ds(start, out.shape[1]), :], out.at[h], sems.at[len(copies)]
                )
            )
    for copy in copies:
        copy.start()
    for copy in copies:
        copy.wait()


def pick(panel, mib, cuts):
    _, width = panel.shape
    outer = lax.axis_size("group") // 4
    outs = [shape((outer, size, width), BF16) for _, _, _, size in cuts]
    sems = pltpu.SemaphoreType.DMA((len(cuts) * outer,))
    return call(
        functools.partial(pick_kernel, [cut[:3] for cut in cuts]),
        mib, [HBM], outs, [sems], panel,
    )


def place(offset, rows, width):
    device = jnp.bitwise_xor(where()[0], offset)
    start = (device & 1) * (width // 2) + (device >> 1) * rows
    return pl.multiple_of(start, rows)


def where():
    member = lax.axis_index("group")
    return lax.axis_index("space"), member & 1, member >> 1 & 1


def write_halves(acc, mine, sent):
    me = where()[0]
    rows = mine.shape[0]
    mine[...] = acc[pl.ds(pl.multiple_of((me & 1) * rows, rows), rows), :]
    sent[...] = acc[pl.ds(pl.multiple_of((1 - (me & 1)) * rows, rows), rows), :]


def halves(width):
    return [shape((width // 2, width), F32)] * 2


def divide_kernel(x, head, tail):
    head[...] = x[:, : head.shape[1], :]
    tail[...] = x[:, head.shape[1] :, :]


def divide(x, part):
    outer, rows, width = x.shape
    outs = [shape((outer, size, width), x.dtype) for size in (part, rows - part)]
    return call(divide_kernel, 4, [VMEM], outs, [], x)


def own_gram_kernel(x_ref, mine, sent, acc):
    step = pl.program_id(0)

    @pl.when(step == 0)
    def _():
        acc[...] = jnp.zeros_like(acc)

    x = x_ref[...]
    acc[...] += dot_t(x, x)

    @pl.when(step == pl.num_programs(0) - 1)
    def _():
        write_halves(acc, mine, sent)


def own_gram(panel):
    rows, width = panel.shape
    tile = rows // 4
    return pl.pallas_call(
        own_gram_kernel,
        grid=(rows // tile,),
        in_specs=[pl.BlockSpec((tile, width), lambda i: (i, 0))],
        out_specs=[pl.BlockSpec((width // 2, width), lambda i: (0, 0))] * 2,
        out_shape=halves(width),
        scratch_shapes=[pltpu.VMEM((width, width), F32)],
        compiler_params=pltpu.CompilerParams(vmem_limit_bytes=48 * 2**20),
        name="own_gram",
    )(panel)


def cross_kernel(begin, level, chained, last, own, other, *refs):
    if chained:
        start, refs = refs[0], refs[1:]
    outs, acc = refs[:-1], refs[-1]
    rows = other.shape[1]

    def add(flip):
        total = start[...] if chained else None
        for h in range(other.shape[0]):
            pair = (own[h, begin : begin + rows, :], other[h])
            part = dot_t(pair[flip], pair[1 - flip])
            total = part if total is None else total + part
        acc[...] = total

    bit = lax.axis_index("group") >> level & 1
    pl.when(bit == 0)(lambda: add(0))
    pl.when(bit == 1)(lambda: add(1))
    if last:
        write_halves(acc, *outs)
    else:
        outs[0][...] = acc[...]


def cross_gram(own, other, begin, level, start, last):
    width = own.shape[-1]
    chained = start is not None
    outs = halves(width) if last else [shape((width, width), F32)]
    return call(
        functools.partial(cross_kernel, begin, level, chained, last),
        8, [VMEM] * (2 + chained), outs,
        [pltpu.VMEM((width, width), F32)],
        own, other, *([start] if chained else []),
    )


def share_kernel(mine, got, *refs):
    outs, acc = refs[:-1], refs[-1]
    acc[...] = mine[...] + got[...]
    rows = outs[0].shape[0]
    for k, out in enumerate(outs):
        start = pl.multiple_of(jnp.bitwise_xor(where()[0] >> 1, k) * rows, rows)
        out[...] = acc[pl.ds(start, rows), :]


def scatter_space(mine, sent):
    chips = lax.axis_size("space") // 2
    rows, width = mine.shape
    got = swap(sent, "space", 1)
    slices = call(
        share_kernel, 4, [VMEM, VMEM],
        [shape((rows // chips, width), F32)] * chips, [pltpu.VMEM((rows, width), F32)],
        mine, got,
    )
    total = slices[0]
    got = [swap(slices[k], "space", 2 * k) for k in range(1, chips)]
    for piece in got:
        total = total + piece
    return total


def gather_space(piece):
    count = lax.axis_size("space")
    pieces = [piece] + [None] * (count - 1)
    for k in range(2, count, 2):
        pieces[k] = swap(piece, "space", k)
    for k in range(0, count, 2):
        pieces[k + 1] = swap(pieces[k], "space", 1)
    return pieces


def assemble_kernel(*refs):
    pieces, out = refs[:-1], refs[-1]
    rows, width = pieces[0].shape[1:]
    for k, piece in enumerate(pieces):
        out[:, pl.ds(place(k, rows, width), rows), :] = piece[...]


def assemble(pieces):
    lead, rows, width = pieces[0].shape
    return call(
        assemble_kernel, 4, [VMEM] * len(pieces),
        [shape((lead, rows * len(pieces), width), F32)], [], *pieces,
    )[0]


def run_filter(pairs, diag, given, pieces, gram, iterate):
    rows, width = pieces[0].shape[1:]
    full = 2 * width
    for p in range(pairs):
        gram[p, :width, :width] = diag[2 * p]
        gram[p, width:, width:] = diag[2 * p + 1]
        for k, piece in enumerate(pieces):
            gram[p, pl.ds(place(k, rows, width), rows), width:] = piece[p]
        gram[p, width:, :width] = gram[p, :width, width:].T
    eye = lax.broadcasted_iota(jnp.int32, (full, full), 0) == lax.broadcasted_iota(
        jnp.int32, (full, full), 1
    )
    for p in range(pairs):
        whole = gram[p]
        trace = jnp.sum(jnp.where(eye, whole, 0.0), keepdims=True)
        shifted = whole / (trace / full) - jnp.where(eye, 1.0, 0.0)
        norm = jnp.sqrt(jnp.sum(shifted * shifted, keepdims=True))
        iterate[p] = shifted / (1.0 + norm)

    def step(_, carry):
        xs = [iterate[p] for p in range(pairs)]
        short = [x.astype(BF16) for x in xs]
        squares = [dot(x, x).astype(BF16) for x in short]
        for p in range(pairs):
            iterate[p] = 1.5 * xs[p] - 0.5 * dot(short[p], squares[p])
        return carry

    lax.fori_loop(0, STEPS - 1, step, 0)
    given_parts = split(given)
    parts = [split(iterate[p]) for p in range(pairs)]
    first = [dot3(part, given_parts) for part in parts]
    second = [dot3(part, split(t)) for part, t in zip(parts, first)]
    third = [dot3(part, split(t)) for part, t in zip(parts, second)]
    mixes = []
    for p in range(pairs):
        applied = 1.5 * first[p] - 0.5 * third[p]
        mixes.append((0.5 * (given + applied)).astype(BF16))
    return mixes


def pair_filter_kernel(diag, sketch, *refs):
    pieces, (mix_ref, gram, iterate) = refs[:-3], refs[-3:]
    mixes = run_filter(2, diag, sketch[0], pieces, gram, iterate)
    for p in range(2):
        mix_ref[p] = mixes[p].reshape(mix_ref.shape[1:])


def pair_filter(diag, pieces, sketch):
    pairs, _, width = pieces[0].shape
    outs = [shape((pairs, 2, width, width), BF16), shape((pairs, 2 * width, 2 * width), F32)]
    return call(
        pair_filter_kernel, 20, [VMEM] * (2 + len(pieces)), outs,
        [pltpu.VMEM((pairs, 2 * width, 2 * width), F32)],
        diag, sketch, *pieces,
    )


def next_diag_kernel(gram, mix, out):
    for p in range(out.shape[0]):
        gh, gl = split(gram[p])
        m = mix[p].reshape(gh.shape[0], -1)
        th, tl = split(dot(gh, m) + dot(gl, m))
        out[p] = dot_t(m, th) + dot_t(m, tl)


def next_diag(gram, mix):
    pairs, _, width, _ = mix.shape
    return call(
        next_diag_kernel, 12, [VMEM] * 2, [shape((pairs, width, width), F32)], [],
        gram, mix,
    )[0]


def read(pieces, h, begin, size):
    for piece in pieces:
        if begin < piece.shape[1]:
            return piece[h, begin : begin + size, :]
        begin -= piece.shape[1]


def merge_own_kernel(mix, mine, near_head, near_tail, out):
    _, bit0, bit1 = where()
    tile = math.gcd(512, near_head.shape[1], near_tail.shape[1])
    for h in range(mine.shape[0]):
        for b in range(0, mine.shape[1], tile):
            total = dot(mine[h, b : b + tile, :], mix[bit1, bit0])
            total += dot(read([near_head, near_tail], h, b, tile), mix[bit1, 1 - bit0])
            out[h, b : b + tile, :] = total.astype(BF16)


def merge_own(mix, mine, *near):
    return call(
        merge_own_kernel, 8, [VMEM] * 4, [shape(mine.shape, BF16)], [],
        mix, mine, *near,
    )[0]


def merge_other_kernel(begin, segments, chained, mix, own, keep, risen, *refs):
    count = len(segments)
    left, passed, refs = refs[:count], refs[count : 2 * count], refs[2 * count :]
    if chained:
        start, refs = refs[0], refs[1:]
    out, *outs, acc = refs
    _, bit0, bit1 = where()
    pair = 1 - bit1
    acc[...] = start[...] if chained else jnp.zeros(acc.shape, F32)
    outer, total_rows, _ = out.shape

    def merge(outer_of, inner_of):
        at = 0
        for k, (skip, rows) in enumerate(segments):
            for h in range(outer):
                total = dot(outer_of(k, h, skip, rows, at), mix[pair, pair])
                total += dot(inner_of(k, h, skip, rows, at), mix[pair, 1 - pair])
                out[h, at : at + rows, :] = total.astype(BF16)
            at += rows

    def near():
        merge(
            lambda k, h, skip, rows, at: left[k][h, skip : skip + rows, :],
            lambda k, h, skip, rows, at: keep[h, at : at + rows, :],
        )

    def distant():
        merge(
            lambda k, h, skip, rows, at: risen[h, at : at + rows, :],
            lambda k, h, skip, rows, at: passed[k][h, skip : skip + rows, :],
        )

    pl.when(bit0 != bit1)(near)
    pl.when(bit0 == bit1)(distant)

    def add(flip):
        for h in range(outer):
            both = (own[h, begin : begin + total_rows, :], out[h])
            acc[...] += dot_t(both[flip], both[1 - flip])

    pl.when(bit1 == 0)(lambda: add(0))
    pl.when(bit1 == 1)(lambda: add(1))
    if chained:
        write_halves(acc, *outs)
    else:
        outs[0][...] = acc[...]


def merge_other(begin, segments, start, mix, own, keep, risen, left, passed):
    outer, _, width = own.shape
    chained = start is not None
    outs = halves(width) if chained else [shape((width, width), F32)]
    args = [mix, own, keep, risen, *left, *passed] + ([start] if chained else [])
    rows = sum(size for _, size in segments)
    return call(
        functools.partial(merge_other_kernel, begin, segments, chained), 12,
        [VMEM] * len(args), [shape((outer, rows, width), BF16)] + outs,
        [pltpu.VMEM((width, width), F32)], *args,
    )


def merge_filter_kernel(level, last, cuts, diag, sketch, own, *refs):
    others, refs = refs[:cuts], refs[cuts:]
    count = 5 if last else 6
    pieces, (out, *refs, stage, sems) = refs[:-count], refs[-count:]
    gram, iterate = refs[-2:]
    mix = run_filter(1, diag, sketch[level], pieces, gram, iterate)[0]
    width = diag.shape[-1]
    bit = lax.axis_index("group") >> level & 1
    tiles = []
    for other in others:
        begin = tiles[-1][2] + tiles[-1][3] if tiles else 0
        size = math.gcd(512, other.shape[1]) if other.shape[1] <= 512 else other.shape[1] // 2
        for skip in range(0, other.shape[1], size):
            tiles.append((other, skip, begin + skip, size))
    copies = []
    for _, _, begin, size in tiles:
        for h in range(own.shape[0]):
            here = pl.ds(begin, size)
            copies.append(
                pltpu.make_async_copy(
                    stage.at[h, here, :], out.at[h, here, :], sems.at[len(copies)]
                )
            )

    def finish(own_mix, other_mix):
        for k, (other, skip, begin, size) in enumerate(tiles):
            for h in range(own.shape[0]):
                total = dot(own[h, begin : begin + size, :], own_mix)
                total += dot(other[h, skip : skip + size, :], other_mix)
                stage[h, begin : begin + size, :] = total.astype(BF16)
                copies[k * own.shape[0] + h].start()

    pl.when(bit == 0)(lambda: finish(mix[:width], mix[width:]))
    pl.when(bit == 1)(lambda: finish(mix[width:], mix[:width]))
    if not last:
        refs[0][0] = mix.reshape(refs[0].shape[1:])
    for copy in copies:
        copy.wait()


def merge_filter(level, last, diag, pieces, sketch, own, others):
    width = diag.shape[-1]
    square = (1, 2 * width, 2 * width)
    outs = [shape(own.shape, BF16)]
    scratch = [pltpu.VMEM(square, F32)] * 2
    if not last:
        outs += [shape((1, 2, width, width), BF16), shape(square, F32)]
        scratch = scratch[:1]
    count = own.shape[0] * 4 * len(others)
    scratch += [pltpu.VMEM(own.shape, BF16), pltpu.SemaphoreType.DMA((count,))]
    return pl.pallas_call(
        functools.partial(merge_filter_kernel, level, last, len(others)),
        in_specs=[VMEM] * (3 + len(others) + len(pieces)),
        out_specs=[HBM] + [VMEM] * (len(outs) - 1),
        out_shape=outs,
        scratch_shapes=scratch,
        compiler_params=pltpu.CompilerParams(vmem_limit_bytes=20 * 2**20),
        name="merge_filter",
    )(diag, sketch, own, *others, *pieces)


def compute(snapshot_basis, sketch):
    rows, width = snapshot_basis.shape
    groups = lax.axis_size("group")
    levels = groups.bit_length() - 1
    member = lax.axis_index("group")
    bit1 = member >> 1 & 1
    block_rows = rows // groups
    cut = block_rows * 3 // 4
    tail = block_rows - cut
    part = block_rows * 3 // 8

    middle, forward, rise, leave = [], [], [], []
    for base in range(0, groups, 4):
        middle += [(base + 1, base + 2), (base + 2, base + 1)]
        forward += [(base + 1, base), (base + 2, base + 3)]
        rise += [(base + 1, base + 3), (base + 2, base)]
        leave += [(base, base + 2), (base + 3, base + 1)]
    pair = [(i, i ^ 1) for i in range(groups)]

    far_own, across = pick(snapshot_basis, 48, [(1, 1, 0, block_rows), (1, 0, 0, block_rows)])
    far = send(far_own, pair)
    pass_on = send(across, middle)
    cuts = [(0, 1, 0, cut), (0, 1, cut, tail), (0, 0, 0, block_rows), (1, 0, 0, cut),
            (1, 0, cut, tail)]
    near_own, tail_own, mine, leave_head, leave_tail = pick(
        after(snapshot_basis, far_own), 48, cuts
    )

    own_halves = own_gram(snapshot_basis)
    own_sum = scatter_space(*own_halves)
    turned = [own_sum] + [swap(own_sum, "group", k) for k in (1, 2, 3)]

    near_head = send(after(near_own, own_sum), pair)
    keep = send(after(far_own, own_sum), middle)
    near_tail = send(after(tail_own, own_sum), pair)
    far_head, far_tail = divide(far, part)
    rise_head = send(after(far_head, own_sum), rise)

    quad = member & 3
    stacked = jnp.stack(turned)
    diag_slices = jnp.stack(
        [lax.dynamic_index_in_dim(stacked, quad ^ g, 0, keepdims=False) for g in range(4)]
    )
    diag = assemble(gather_space(diag_slices))

    cross = cross_gram(across, far, 0, 0, None, False)[0]
    cross = cross_gram(mine, near_head, 0, 0, cross, False)[0]
    cross_halves = cross_gram(mine, near_tail, cut, 0, cross, True)
    cross_sum = scatter_space(*cross_halves)
    one, two, three = [swap(cross_sum, "group", k) for k in (1, 2, 3)]
    here = cross_sum + one
    there = two + three
    both = jnp.stack([jnp.where(bit1 == 0, here, there), jnp.where(bit1 == 0, there, here)])

    pass_parts = divide(pass_on, cut)
    left_head = send(after(leave_head, cross_sum), leave)
    pass_head = send(after(pass_parts[0], cross_sum), forward)
    rise_tail = send(after(far_tail, cross_sum), rise)
    left_tail = send(after(leave_tail, cross_sum), leave)
    pass_tail = send(after(pass_parts[1], cross_sum), forward)

    mix, gram = pair_filter(diag, gather_space(both), sketch)
    diag = next_diag(gram, mix)
    own_merged = merge_own(mix, mine, near_head, near_tail)
    args = [mix, own_merged]
    keep_head, keep_tail = divide(keep, part)
    other_head, cross = merge_other(
        0, [(0, part)], None, *args, keep_head, rise_head, [left_head], [pass_head]
    )
    other_tail, *both_halves = merge_other(
        part, [(part, cut - part), (0, tail)], cross, *args, keep_tail, rise_tail,
        [left_head, left_tail], [pass_head, pass_tail],
    )
    total = scatter_space(*both_halves)
    one, two, three = [swap(total, "group", k) for k in (1, 2, 3)]
    total = (total + one) + (two + three)
    result = merge_filter(
        1, levels == 2, diag, gather_space(total[None]), sketch,
        own_merged, [other_head, other_tail],
    )

    for level in range(2, levels):
        merged = result[0]
        bit = member >> level & 1
        pairs = merged.reshape(-1, 2, block_rows, width)
        kept = lax.dynamic_index_in_dim(pairs, bit, 1, keepdims=False)
        given = lax.dynamic_index_in_dim(pairs, 1 - bit, 1, keepdims=False)
        got = swap(given, "group", 1 << level)
        diag_own = next_diag(result[2], result[1])[0]
        diag_got = swap(diag_own, "group", 1 << level)
        total = scatter_space(*cross_gram(kept, got, 0, level, None, True))
        for low in range(level + 1):
            total = total + swap(total, "group", 1 << low)
        diag = jnp.stack(
            [jnp.where(bit == 0, diag_own, diag_got), jnp.where(bit == 0, diag_got, diag_own)]
        )
        result = merge_filter(
            level, level + 1 == levels, diag, gather_space(total[None]),
            sketch, kept, [got],
        )
    return result[0].reshape(block_rows, width)


def solution(mesh):
    in_specs = (P("space", "group"), P())
    out_specs = P(("space", "group"), None)
    return jax.shard_map(compute, mesh=mesh, in_specs=in_specs, out_specs=out_specs, check_vma=False)
```
